512 devices in a mesh: pair: 32 (over y, x, core), aux: 16 (over z).
Axes of the slice: x: 4, y: 4, z: 16, core: 2. Of those that a mesh axis runs over, the one named last changes fastest.
Arguments:
- integrals: bfloat16 [8192, 256, 64], P(('pair', 'aux')), may hold values from -6 to 6
- amplitudes: bfloat16 [8192, 64, 64], P(('pair', 'aux')), may hold values from -0.75 to 0.75
- pno_density: bfloat16 [8192, 64, 64], P(('pair', 'aux')), may hold values from -6 to 6
- pno_coef: bfloat16 [8192, 256, 64], P(('pair', 'aux')), may hold values from -0.75 to 0.75
- pao_blocks: int32 [8192, 2], P(('pair', 'aux')), may hold values from 0 to 5, all different within a row
- aux_slice: int32 [8192, 2], P(('pair', 'aux')), may hold values from 0 to 15, all different within a row; in each aligned block of 16 rows (0 to 15, 16 to 31, ...) at most 4 rows name the same one
- aux_offset: int32 [8192, 2], P(('pair', 'aux')), may hold values from 0 to 3
Outputs:
- aux_density: float32 [8192, 768], P('aux', 'pair')
- virtual_density: float32 [768, 768], P('aux', 'pair')
The draws below stay inside these ranges and needn't reach their ends.
Inputs may be any that keep to these rules, and one draw needn't show every extreme that they name: `pao_blocks`: the 2 blocks of a pair are different. `aux_slice`: the 2 slices of a pair are different; among the pairs of one device no slice is named more than 4 times, and in every draw some device names some slice exactly 4 times.
All inputs are finite; a program needn't handle non-finite values.
Results may differ from the reference program's by a relative error of at most 0.0041.
Values may be sent and summed in bfloat16 or wider, within the bound.
No kernel may reach another device: no remote copies, remote signals or barrier semaphores. Data moves between devices by JAX's collectives and lax.ppermute only.
A program may use at most 64 MiB of HBM per device.

```python
import math
import jax
import jax.numpy as jnp
import numpy as np
from jax import lax

NPNO = 64
ABLK = 128
PBLK = 128
DOMB = 2
ADOM = 2
NBLK = 6
ABPO = 4
PAIR_DEV = 16
PAIRS = 8192
CAP = 4
N_PAIR = 32
N_AUX = 16


def touch_ends(drawn, rng, least, top_value):
    place = [jax.random.randint(jax.random.fold_in(rng, axis), (), 0, length) for axis, length in enumerate(drawn.shape)]
    longest = drawn.shape.index(max(drawn.shape))
    next_to = place[:longest] + [(place[longest] + 1) % drawn.shape[longest]] + place[longest + 1:]
    return drawn.at[tuple(place)].set(least).at[tuple(next_to)].set(top_value)


def block_levels(own_key, dims, shards, low, largest):
    def one(position, shards_of):
        heights = jax.random.uniform(jax.random.fold_in(jax.random.fold_in(own_key, 6), position), (shards_of,), jnp.float32, low / len(shards), largest / len(shards))
        return jnp.repeat(jnp.exp(heights), dims[position] // shards_of).reshape((-1,) + (1,) * (len(dims) - position - 1))

    factor_of = one(*shards[0])
    for cut in shards[1:]:
        factor_of = factor_of * one(*cut)
    return factor_of


def different_ones(stream_key, rows, count, top, lift):
    order = jax.random.permutation(jax.random.fold_in(stream_key, 1), count)
    pull = order
    for power in range(3):
        pull = pull * pull // count
    pull = pull * lift // count
    tickets = jax.random.randint(jax.random.fold_in(stream_key, 2), (rows, count), 0, 4096) + pull
    holders = jax.random.permutation(jax.random.fold_in(stream_key, 3), rows)[jnp.arange(count) % rows]
    tickets = jnp.where(jnp.arange(rows)[:, None] == holders[None, :], 1 << 14, tickets)
    score = tickets * count + jnp.arange(count)
    return lax.top_k(score.astype(jnp.int32), top)[1].astype(jnp.int32)


def routed_block(rng, own, number, rows, number_of, top, reach, slope):
    ranking = jax.random.permutation(rng, number_of)
    heavy_load, usual = load_shares(number_of, rows * top, reach, slope, True), load_shares(number_of, rows * top, reach, slope, False)
    places = jnp.arange(number_of)

    def named(sizes, offset_by):
        used = int((sizes > 0).sum())
        fixed = max(1, used // 4)
        moved = fixed + (places - fixed + offset_by * (used - fixed)) % max(1, number_of - fixed)
        return jnp.zeros((number_of,), jnp.int32).at[ranking[jnp.where(places < fixed, places, moved)]].set(jnp.asarray(sizes, jnp.int32))

    sizes = jnp.where(number % 4 == 0, named(heavy_load, number // 4), named(usual, number - number // 4 - 1))
    mixed = jax.random.permutation(jax.random.fold_in(own, 3), number_of)
    source_of, taker = mixed[0:number_of // 2 * 2:2], mixed[1:number_of // 2 * 2:2]
    room = jnp.minimum(sizes[source_of] - 1, reach - sizes[taker]) // 2
    room = jnp.where((source_of == ranking[0]) | (taker == ranking[0]) | (sizes[taker] == 0), 0, jnp.maximum(room, 0))
    moved = jax.random.randint(jax.random.fold_in(own, 4), (number_of // 2,), 0, 1 << 20) % (room + 1)
    sizes = sizes.at[source_of].add(-moved).at[taker].add(moved)
    members = jnp.searchsorted(jnp.cumsum(sizes), jnp.arange(rows * top), side="right").astype(jnp.int32)
    listing = members.reshape(top, rows).T
    listing = listing[jax.random.permutation(jax.random.fold_in(own, 1), rows)]
    offset_by = jax.random.randint(jax.random.fold_in(own, 2), (rows, 1), 0, top)
    return jnp.take_along_axis(listing, (jnp.arange(top)[None, :] + offset_by) % top, axis=1)


def load_shares(number_of, total, bound, skew, full):
    loads = [(1 << 20) // math.isqrt(grade ** skew) + 1 for grade in range(1, number_of + 1)]
    largest = bound if full else min(bound, max(-(-total // number_of), total * loads[0] // sum(loads)))
    least = 1 if total - largest >= number_of - 1 else 0
    holding, surplus = [largest] + [least] * (number_of - 1), total - largest - least * (number_of - 1)
    while surplus > 0:
        free = [i for i in range(1, number_of) if holding[i] < largest] or [i for i in range(1, number_of) if holding[i] < bound]
        whole, left = sum([loads[i] for i in free]), surplus
        for i in free:
            addition = min(bound - holding[i], max(1, left * loads[i] // whole), surplus)
            holding[i] = holding[i] + addition
            surplus = surplus - addition
    return np.array(holding)


def scatter_about(own_key, shape, spread, most, cuts=(), kind=jnp.bfloat16):
    values = spread * jax.random.normal(own_key, shape, jnp.float32)
    if cuts:
        values = values * block_levels(own_key, shape, cuts, -0.22, 0.18)
    return jnp.clip(values, -most, most).astype(kind)


def setup_inputs(seed: int = 0) -> dict:
    streams_of = jax.random.split(jax.random.key(seed), 8)
    integrals = scatter_about(streams_of[0], (PAIRS, ADOM * ABLK, NPNO), 1.0, 6.0, ((0, 512),))
    amplitudes = scatter_about(streams_of[1], (PAIRS, NPNO, NPNO), NPNO ** -0.5, 0.75, ((0, 512),))
    pno_density = scatter_about(streams_of[2], (PAIRS, NPNO, NPNO), 1.0, 6.0, ((0, 512),))
    pno_coef = scatter_about(streams_of[3], (PAIRS, DOMB * PBLK, NPNO), NPNO ** -0.5, 0.75, ((0, 512),))
    pao_blocks = different_ones(streams_of[4], PAIRS, NBLK, DOMB, 2730)
    aux_slice_keys = jax.random.split(jax.random.fold_in(streams_of[5], 1), PAIRS // PAIR_DEV)
    aux_slice_turns = jax.random.permutation(jax.random.fold_in(streams_of[5], 3), PAIRS // PAIR_DEV)
    aux_slice = jax.vmap(lambda own, number: routed_block(jax.random.fold_in(streams_of[5], 2), own, number, PAIR_DEV, N_AUX, ADOM, CAP, 2))(aux_slice_keys, aux_slice_turns).reshape((PAIRS, ADOM))
    aux_offset = touch_ends(jax.random.randint(streams_of[6], (PAIRS, ADOM), 0, ABPO), jax.random.fold_in(streams_of[6], 1), 0, ABPO - 1).astype(jnp.int32)
    return dict(integrals=integrals, amplitudes=amplitudes, pno_density=pno_density, pno_coef=pno_coef, pao_blocks=pao_blocks, aux_slice=aux_slice, aux_offset=aux_offset)


def reference(integrals, amplitudes, pno_density, pno_coef, pao_blocks, aux_slice, aux_offset):
    block_pairs = PAIR_DEV * N_AUX
    out_scale = 1.0 / math.sqrt(PAIR_DEV * N_PAIR)

    def add_block(carry, block_index):
        gamma_acc, virt_acc = carry
        first = (block_index * block_pairs).astype(jnp.int32)

        def take(array):
            return lax.dynamic_slice_in_dim(array, first, block_pairs, 0)
        block_ints = take(integrals).astype(jnp.float32)
        block_amps = take(amplitudes).astype(jnp.float32)
        block_dens = take(pno_density).astype(jnp.float32)
        block_coef = take(pno_coef).astype(jnp.float32)
        block_pao = take(pao_blocks)
        block_rows = take(aux_slice) * ABPO + take(aux_offset)
        three_index = jnp.einsum('pqr,prs->pqs', block_ints, block_amps).astype(jnp.bfloat16)
        three_index = lax.optimization_barrier(three_index).astype(jnp.float32)
        pao_pieces = jnp.einsum('pqs,pys->pqy', three_index, block_coef).astype(jnp.bfloat16)
        pao_pieces = lax.optimization_barrier(pao_pieces).astype(jnp.float32)
        pieces = pao_pieces.reshape(block_pairs, ADOM, ABLK, DOMB, PBLK).transpose(0, 1, 3, 2, 4)
        gamma_acc = gamma_acc.at[block_rows[:, :, None], :, block_pao[:, None, :], :].add(pieces)
        weighted = jnp.einsum('pyr,prs->pys', block_coef, block_dens).astype(jnp.bfloat16)
        weighted = lax.optimization_barrier(weighted).astype(jnp.float32)
        pair_density = jnp.einsum('pys,pzs->pyz', weighted, block_coef)
        pair_density = pair_density.reshape(block_pairs, DOMB, PBLK, DOMB, PBLK).transpose(0, 1, 3, 2, 4)
        virt_acc = virt_acc.at[block_pao[:, :, None], :, block_pao[:, None, :], :].add(pair_density)
        return ((gamma_acc, virt_acc), None)
    gamma_init = jnp.zeros((N_AUX * ABPO, ABLK, NBLK, PBLK), jnp.float32)
    virt_init = jnp.zeros((NBLK, PBLK, NBLK, PBLK), jnp.float32)
    (gamma_acc, virt_acc), _ = lax.scan(add_block, (gamma_init, virt_init), jnp.arange(N_PAIR, dtype=jnp.int32))
    aux_density = gamma_acc.reshape(N_AUX * ABPO * ABLK, NBLK * PBLK) * out_scale
    virtual_density = virt_acc.reshape(NBLK * PBLK, NBLK * PBLK) * out_scale
    return (aux_density, virtual_density)
```

```python
import math

import jax
import jax.numpy as jnp
from jax import lax
from jax.experimental import pallas as pl
from jax.experimental.pallas import tpu as pltpu
from jax.sharding import Mesh
from jax.sharding import PartitionSpec as P

NBLK = 6
ABPO = 4
BF = jnp.bfloat16
F32 = jnp.float32
PAIRS = 16
GROUP = 64
ROWS1 = 208
ROWS2 = 120
ROWS3 = 24
VMEM = pltpu.CompilerParams(vmem_limit_bytes=56 * 1024 * 1024)


def dot00(a, b):
    return lax.dot_general(a, b, (((0,), (0,)), ((), ())), preferred_element_type=F32)


def dot10(a, b):
    return lax.dot_general(a, b, (((1,), (0,)), ((), ())), preferred_element_type=F32)


def local_kernel(
    blocks, owners, offsets, ints, amps, dens, coef, out, pieces, weighted_rows, coef_rows, virt
):
    weighted_rows[...] = jnp.zeros(weighted_rows.shape, BF)
    coef_rows[...] = jnp.zeros(coef_rows.shape, BF)
    lane = lax.broadcasted_iota(jnp.int32, (1, 128), 1) % 64
    slice_row = jnp.zeros((1, 128), F32)
    block_row = jnp.zeros((1, 128), F32)
    offset_row = jnp.zeros((1, 128), F32)
    for p in range(PAIRS):
        c = coef[p]
        weighted = dot00(dens[p], c).astype(BF)
        three_index = dot00(amps[p], ints[p]).astype(BF)
        piece = dot00(c, three_index)
        for h in range(2):
            at = pl.ds(pl.multiple_of(blocks[h, p] * 128, 128), 128)
            weighted_rows[64 * p : 64 * p + 64, at] = weighted[:, 128 * h : 128 * h + 128]
            coef_rows[64 * p : 64 * p + 64, at] = c[:, 128 * h : 128 * h + 128]
            for k in range(2):
                slot = 4 * p + 2 * h + k
                pieces[pl.ds(slot, 128, 64), :] = piece[
                    128 * h : 128 * h + 128, 128 * k : 128 * k + 128
                ]
                here = lane == slot
                slice_row = jnp.where(here, owners[k, p].astype(F32), slice_row)
                block_row = jnp.where(here, blocks[h, p].astype(F32), block_row)
                offset_row = jnp.where(here, offsets[k, p].astype(F32), offset_row)
    sub = lax.broadcasted_iota(jnp.int32, (8, 128), 0)
    labels = jnp.where(sub == 0, slice_row, jnp.where(sub == 1, block_row, offset_row))
    virt[...] = dot00(coef_rows[...], weighted_rows[...])
    for g in range(GROUP):
        out[g, 0:128, :] = pieces[128 * g : 128 * g + 128, :].astype(BF)
        first, half = 24 * (g // 2), 384 * (g % 2)
        tiles = [
            virt[first + 8 * i : first + 8 * i + 8, half + 128 * j : half + 128 * j + 128]
            for i in range(3)
            for j in range(3)
        ]
        out[g, 128:ROWS1, :] = jnp.concatenate(tiles + [labels], 0).astype(BF)


def place_kernel(got, out, hot, acc):
    lane = lax.broadcasted_iota(jnp.int32, (1, 128), 1)
    cell = lax.broadcasted_iota(jnp.int32, (384, 128), 0)
    for i in range(GROUP // 2):
        first = got[2 * i, 200:208, :].astype(F32)
        second = got[2 * i + 1, 200:208, :].astype(F32)
        both = jnp.where(lane < 64, first, second)
        target = both[0:1] * 24.0 + both[1:2] * 4.0 + both[2:3]
        hot[:, 128 * i : 128 * i + 128] = (cell == target.astype(jnp.int32)).astype(BF)
    data = jnp.concatenate(
        [got[:, 0:64, :].reshape(4096, 128), got[:, 64:128, :].reshape(4096, 128)], 1
    )
    acc[...] = dot10(hot[...], data)
    total = got[0, 128:200, :].astype(F32)
    for g in range(1, GROUP):
        total = total + got[g, 128:200, :].astype(F32)
    lanes8 = lax.broadcasted_iota(jnp.int32, (8, 128), 1)
    windows = [[], [], [], []]
    for i in range(3):
        a, b, c = (total[24 * i + 8 * j : 24 * i + 8 * j + 8] for j in range(3))
        windows[0].append(a)
        windows[1].append(jnp.where(lanes8 < 32, pltpu.roll(a, 32, 1), pltpu.roll(b, 32, 1)))
        windows[2].append(jnp.where(lanes8 < 64, pltpu.roll(b, 64, 1), pltpu.roll(c, 64, 1)))
        windows[3].append(pltpu.roll(c, 96, 1))
    for z in range(8):
        rows = [acc[48 * z : 48 * z + 48, 0:128], acc[48 * z : 48 * z + 48, 128:256]]
        out[z] = jnp.concatenate(rows + windows[z % 4], 0).astype(BF)


def column_kernel(place, got, out):
    total = got[0].astype(F32)
    for z in range(1, 8):
        total = total + got[z].astype(F32)
    sub = lax.broadcasted_iota(jnp.int32, (8, 128), 0)
    lane = lax.broadcasted_iota(jnp.int32, (8, 128), 1)
    tiles = []
    for i in range(6):
        a, b = total[8 * i : 8 * i + 8], total[48 + 8 * i : 56 + 8 * i]
        tiles.append(jnp.where(sub < 4, a, pltpu.roll(b, 4, 0)))
        tiles.append(jnp.where(sub < 4, pltpu.roll(a, 4, 0), b))
    column = 2 * place[0]
    virt = [total[96:104], total[104:112], total[112:120]]
    for low in range(2):
        v0, v1, v2 = virt
        if low:
            v0, v1, v2 = (pltpu.roll(v, 80, 1) for v in virt)
        packed = [jnp.where(lane < 64, v0, pltpu.roll(v1, 64, 1)), v2]
        for p in range(32):
            b_first, b_last = (24 * p) // 128, (24 * p + 23) // 128
            tile = tiles[6 * low + b_first]
            if b_last != b_first:
                tile = jnp.where(column >= 24 * p - 128 * b_first, tile, tiles[6 * low + b_last])
            out[2 * p + low] = jnp.concatenate([tile] + packed, 0).astype(BF)


def final_kernel(place, got, aux_out, virt_out, *, scale):
    p = place[0]
    for j in range(12):
        tile = got[lax.rem(12 * p + j, 64), 0:8, :].astype(F32) * scale
        for y in range(2):
            for o in range(ABPO):
                aux_out[2 * j + y : 2 * j + y + 1, 128 * o : 128 * o + 128] = tile[
                    4 * y + o : 4 * y + o + 1
                ]
    both = got[2 * p + place[1], 8:24, :].astype(F32) * scale
    virt_out[0:8, :] = both[0:8, 0:48]
    virt_out[8:16, :] = pltpu.roll(both[0:8], 64, 1)[:, 0:48]
    virt_out[16:24, :] = both[8:16, 0:48]


def call(body, ins, outs, scalars, scratch=()):
    smem = pl.BlockSpec(memory_space=pltpu.SMEM)
    vmem = pl.BlockSpec(memory_space=pltpu.VMEM)
    return pl.pallas_call(
        body,
        in_specs=[smem] * len(scalars) + [vmem] * len(ins),
        out_specs=[vmem] * len(outs),
        out_shape=outs,
        scratch_shapes=scratch,
        compiler_params=VMEM,
    )(*scalars, *ins)


def on_device(integrals, amplitudes, pno_density, pno_coef, pao_blocks, aux_slice, aux_offset):
    pair = lax.axis_index("pair")
    low = lax.axis_index("low")
    high = lax.axis_index("high")
    scale = 1.0 / math.sqrt(PAIRS * 32)
    sds = jax.ShapeDtypeStruct
    (sent,) = call(
        local_kernel,
        [
            jnp.swapaxes(integrals, 1, 2),
            amplitudes,
            pno_density,
            jnp.swapaxes(pno_coef, 1, 2),
        ],
        [sds((GROUP, ROWS1, 128), BF)],
        [pao_blocks.T, aux_slice.T, aux_offset.T],
        [
            pltpu.VMEM((8192, 128), F32),
            pltpu.VMEM((1024, 768), BF),
            pltpu.VMEM((1024, 768), BF),
            pltpu.VMEM((768, 768), F32),
        ],
    )
    got = lax.all_to_all(sent, ("pair", "low"), split_axis=0, concat_axis=0, tiled=True)
    (sent,) = call(
        place_kernel,
        [got],
        [sds((8, ROWS2, 128), BF)],
        [],
        [pltpu.VMEM((384, 4096), BF), pltpu.VMEM((384, 256), F32)],
    )
    got = lax.all_to_all(sent, "high", split_axis=0, concat_axis=0, tiled=True)
    (sent,) = call(
        column_kernel, [got], [sds((GROUP, ROWS3, 128), BF)], [(2 * pair + low).reshape(1)]
    )
    got = lax.all_to_all(sent, ("pair", "low"), split_axis=0, concat_axis=0, tiled=True)
    aux, virt = call(
        lambda *refs: final_kernel(*refs, scale=scale),
        [got],
        [sds((24, 512), F32), sds((24, 48), F32)],
        [jnp.stack([pair, high // 4]).astype(jnp.int32)],
    )
    return aux.T, virt.T


def solution(mesh):
    split = Mesh(mesh.devices.reshape(32, 8, 2), ("pair", "high", "low"))
    every = ("pair", "high", "low")
    in_specs = (P(every, None, None),) * 4 + (P(every, None),) * 3
    out_specs = (P(("high", "low"), "pair"),) * 2
    return jax.shard_map(
        on_device, mesh=split, in_specs=in_specs, out_specs=out_specs, check_vma=False
    )
```

```python
import math

import jax
import jax.numpy as jnp
from jax import lax
from jax.experimental import pallas as pl
from jax.experimental.pallas import tpu as pltpu
from jax.sharding import Mesh
from jax.sharding import PartitionSpec as P

NBLK = 6
ABPO = 4
BF = jnp.bfloat16
F32 = jnp.float32
PAIRS = 16
GROUP = 64
ROWS1 = 168
ROWS2 = 112
ROWS3 = 16
VMEM = pltpu.CompilerParams(vmem_limit_bytes=40 * 1024 * 1024)


def dot00(a, b):
    return lax.dot_general(a, b, (((0,), (0,)), ((), ())), preferred_element_type=F32)


def dot10(a, b):
    return lax.dot_general(a, b, (((1,), (0,)), ((), ())), preferred_element_type=F32)


def virtual_kernel(blocks, core, dens, coef, mine, other, weighted_rows, coef_rows):
    weighted_rows[...] = jnp.zeros(weighted_rows.shape, BF)
    coef_rows[...] = jnp.zeros(coef_rows.shape, BF)
    for p in range(PAIRS):
        c = coef[p]
        weighted = dot00(dens[p], c).astype(BF)
        for h in range(2):
            at = pl.ds(pl.multiple_of(blocks[h, p] * 128, 128), 128)
            weighted_rows[64 * p : 64 * p + 64, at] = weighted[:, 128 * h : 128 * h + 128]
            coef_rows[64 * p : 64 * p + 64, at] = c[:, 128 * h : 128 * h + 128]
    left = coef_rows[...]
    other_half = pl.ds(pl.multiple_of(384 * (1 - core[0]), 128), 384)
    other[...] = dot00(left, weighted_rows[:, other_half]).astype(BF)
    my_half = pl.ds(pl.multiple_of(384 * core[0], 128), 384)
    mine[...] = dot00(left, weighted_rows[:, my_half])


def piece_kernel(ints, amps, coef, out, pieces, rounded, sems):
    for p in range(PAIRS):
        three_index = dot00(amps[p], ints[p]).astype(BF)
        piece = dot00(coef[p], three_index)
        for h in range(2):
            for k in range(2):
                pieces[pl.ds(4 * p + 2 * h + k, 128, 64), :] = piece[
                    128 * h : 128 * h + 128, 128 * k : 128 * k + 128
                ]
    copies = []
    for i in range(8):
        for g in range(8 * i, 8 * i + 8):
            rounded[g] = pieces[128 * g : 128 * g + 128, :].astype(BF)
        copies.append(
            pltpu.make_async_copy(
                rounded.at[8 * i : 8 * i + 8], out.at[8 * i : 8 * i + 8, 0:128], sems.at[i]
            )
        )
        copies[-1].start()
    for copy in copies:
        copy.wait()


def rest_kernel(blocks, owners, offsets, filled, mine, other, out, rows, sem):
    lane = lax.broadcasted_iota(jnp.int32, (1, 128), 1) % 64
    slice_row = jnp.zeros((1, 128), F32)
    block_row = jnp.zeros((1, 128), F32)
    offset_row = jnp.zeros((1, 128), F32)
    for p in range(PAIRS):
        for h in range(2):
            for k in range(2):
                here = lane == 4 * p + 2 * h + k
                slice_row = jnp.where(here, owners[k, p].astype(F32), slice_row)
                block_row = jnp.where(here, blocks[h, p].astype(F32), block_row)
                offset_row = jnp.where(here, offsets[k, p].astype(F32), offset_row)
    sub = lax.broadcasted_iota(jnp.int32, (8, 128), 0)
    top = sub < 4
    labels = jnp.where(sub == 4, slice_row, jnp.where(sub == 5, block_row, offset_row))
    for i in range(GROUP // 2):
        both = mine[24 * i : 24 * i + 24, :] + other[24 * i : 24 * i + 24, :].astype(F32)
        first = [both[0:8, 128 * j : 128 * j + 128] for j in range(3)]
        mid = [both[8:16, 128 * j : 128 * j + 128] for j in range(3)]
        last = [both[16:24, 128 * j : 128 * j + 128] for j in range(3)]
        moved = [pltpu.roll(m, 4, 0) for m in mid]
        even = first + [jnp.where(top, mid[0], moved[1]), jnp.where(top, mid[2], labels)]
        odd = last + [jnp.where(top, moved[0], mid[1]), jnp.where(top, moved[2], labels)]
        rows[2 * i] = jnp.concatenate(even, 0).astype(BF)
        rows[2 * i + 1] = jnp.concatenate(odd, 0).astype(BF)
    copy = pltpu.make_async_copy(rows, out.at[:, 128:ROWS1], sem)
    copy.start()
    copy.wait()


def place_kernel(got, out, hot, acc):
    lane = lax.broadcasted_iota(jnp.int32, (1, 128), 1)
    cell = lax.broadcasted_iota(jnp.int32, (384, 128), 0)
    for i in range(GROUP // 2):
        first = got[2 * i, 160:168, :].astype(F32)
        second = got[2 * i + 1, 160:168, :].astype(F32)
        both = jnp.where(lane < 64, first, second)
        target = both[4:5] * 24.0 + both[5:6] * 4.0 + both[6:7]
        hot[:, 128 * i : 128 * i + 128] = (cell == target.astype(jnp.int32)).astype(BF)
    data = jnp.concatenate(
        [got[:, 0:64, :].reshape(4096, 128), got[:, 64:128, :].reshape(4096, 128)], 1
    )
    acc[...] = dot10(hot[...], data)
    lanes8 = lax.broadcasted_iota(jnp.int32, (8, 128), 1)
    for half in range(2):
        mine = [g for g in range(GROUP) if (g // 2) % 2 == half]
        total = got[mine[0], 128:168, :].astype(F32)
        for g in mine[1:]:
            total = total + got[g, 128:168, :].astype(F32)
        whole = [total[0:8], total[8:16], total[16:24]]
        part = [total[24:32], pltpu.roll(total[24:32], 4, 0), total[32:40]]
        for z in range(4):
            at = 4 * half + z
            rows = [acc[48 * at : 48 * at + 48, 0:128], acc[48 * at : 48 * at + 48, 128:256]]
            for a, b, c in (whole, part):
                if z == 0:
                    rows.append(a)
                elif z == 1:
                    rows.append(
                        jnp.where(lanes8 < 32, pltpu.roll(a, 32, 1), pltpu.roll(b, 32, 1))
                    )
                elif z == 2:
                    rows.append(
                        jnp.where(lanes8 < 64, pltpu.roll(b, 64, 1), pltpu.roll(c, 64, 1))
                    )
                else:
                    rows.append(pltpu.roll(c, 96, 1))
            out[at] = jnp.concatenate(rows, 0).astype(BF)


def column_kernel(place, got, out):
    total = got[0].astype(F32)
    for z in range(1, 8):
        total = total + got[z].astype(F32)
    sub = lax.broadcasted_iota(jnp.int32, (8, 128), 0)
    lane = lax.broadcasted_iota(jnp.int32, (8, 128), 1)
    tiles = []
    for i in range(6):
        a, b = total[8 * i : 8 * i + 8], total[48 + 8 * i : 56 + 8 * i]
        tiles.append(jnp.where(sub < 4, a, pltpu.roll(b, 4, 0)))
        tiles.append(jnp.where(sub < 4, pltpu.roll(a, 4, 0), b))
    column = 2 * place[0]
    whole, part = total[96:104], total[104:112]
    packed = [
        jnp.where(lane < 64, whole, pltpu.roll(part, 64, 1)),
        jnp.where(lane < 64, pltpu.roll(whole, 80, 1), pltpu.roll(part, 16, 1)),
    ]
    for low in range(2):
        for p in range(32):
            b_first, b_last = (24 * p) // 128, (24 * p + 23) // 128
            tile = tiles[6 * low + b_first]
            if b_last != b_first:
                tile = jnp.where(column >= 24 * p - 128 * b_first, tile, tiles[6 * low + b_last])
            out[2 * p + low] = jnp.concatenate([tile, packed[low]], 0).astype(BF)


def final_kernel(place, got, aux_out, virt_out, *, scale):
    p = place[0]
    for j in range(12):
        tile = got[lax.rem(12 * p + j, 64), 0:8, :].astype(F32) * scale
        for y in range(2):
            for o in range(ABPO):
                aux_out[2 * j + y : 2 * j + y + 1, 128 * o : 128 * o + 128] = tile[
                    4 * y + o : 4 * y + o + 1
                ]
    sub = lax.broadcasted_iota(jnp.int32, (8, 128), 0)
    first = got[2 * p, 8:16, :].astype(F32) * scale
    last = got[2 * p + 1, 8:16, :].astype(F32) * scale
    mid = jnp.where(sub < 4, pltpu.roll(first, 64, 1), pltpu.roll(pltpu.roll(last, 64, 1), 4, 0))
    virt_out[0:8, :] = first[:, 0:48]
    virt_out[8:16, :] = mid[:, 0:48]
    virt_out[16:24, :] = last[:, 0:48]


def in_vmem(x):
    return pltpu.with_memory_space_constraint(x, pltpu.VMEM)


def call(body, ins, outs, scalars, scratch=(), in_place=None, anywhere=False):
    smem = pl.BlockSpec(memory_space=pltpu.SMEM)
    vmem = pl.BlockSpec(memory_space=pltpu.VMEM)
    hbm = pl.BlockSpec(memory_space=pl.ANY)
    in_specs = [smem] * len(scalars) + [vmem] * len(ins)
    operands = [*scalars, *ins]
    aliases = {}
    if in_place is not None:
        in_specs.insert(len(scalars), hbm)
        operands.insert(len(scalars), in_place)
        aliases = {len(scalars): 0}
    return pl.pallas_call(
        body,
        in_specs=in_specs,
        out_specs=[hbm if anywhere else vmem] * len(outs),
        out_shape=outs,
        scratch_shapes=scratch,
        input_output_aliases=aliases,
        compiler_params=VMEM,
    )(*operands)


def on_device(integrals, amplitudes, pno_density, pno_coef, pao_blocks, aux_slice, aux_offset):
    pair = lax.axis_index("pair")
    low = lax.axis_index("low")
    scale = 1.0 / math.sqrt(PAIRS * 32)
    sds = jax.ShapeDtypeStruct
    coef = jnp.swapaxes(pno_coef, 1, 2)
    blocks = pao_blocks.T
    mine, other = call(
        virtual_kernel,
        [pno_density, coef],
        [sds((768, 384), F32), sds((768, 384), BF)],
        [blocks, (pair % 2).reshape(1)],
        [pltpu.VMEM((1024, 768), BF), pltpu.VMEM((1024, 768), BF)],
    )
    other = lax.ppermute(other, "pair", [(i, i ^ 1) for i in range(32)])
    (filled,) = call(
        piece_kernel,
        [jnp.swapaxes(integrals, 1, 2), amplitudes, coef],
        [sds((GROUP, ROWS1, 128), BF)],
        [],
        [
            pltpu.VMEM((8192, 128), F32),
            pltpu.VMEM((GROUP, 128, 128), BF),
            pltpu.SemaphoreType.DMA((8,)),
        ],
        anywhere=True,
    )
    (sent,) = call(
        rest_kernel,
        [mine, other],
        [sds((GROUP, ROWS1, 128), BF)],
        [blocks, aux_slice.T, aux_offset.T],
        [pltpu.VMEM((GROUP, ROWS1 - 128, 128), BF), pltpu.SemaphoreType.DMA(())],
        in_place=filled,
        anywhere=True,
    )
    got = lax.all_to_all(sent, ("pair", "low"), split_axis=0, concat_axis=0, tiled=True)
    (sent,) = call(
        place_kernel,
        [in_vmem(got)],
        [sds((8, ROWS2, 128), BF)],
        [],
        [pltpu.VMEM((384, 4096), BF), pltpu.VMEM((384, 256), F32)],
    )
    got = lax.all_to_all(sent, "high", split_axis=0, concat_axis=0, tiled=True)
    (sent,) = call(
        column_kernel,
        [in_vmem(got)],
        [sds((GROUP, ROWS3, 128), BF)],
        [(2 * pair + low).reshape(1)],
    )
    got = lax.all_to_all(sent, ("pair", "low"), split_axis=0, concat_axis=0, tiled=True)
    aux, virt = call(
        lambda *refs: final_kernel(*refs, scale=scale),
        [in_vmem(got)],
        [sds((24, 512), F32), sds((24, 48), F32)],
        [pair.reshape(1)],
    )
    return aux.T, virt.T


def solution(mesh):
    split = Mesh(mesh.devices.reshape(32, 8, 2), ("pair", "high", "low"))
    every = ("pair", "high", "low")
    in_specs = (P(every, None, None),) * 4 + (P(every, None),) * 3
    out_specs = (P(("high", "low"), "pair"),) * 2
    return jax.shard_map(
        on_device, mesh=split, in_specs=in_specs, out_specs=out_specs, check_vma=False
    )
```

```python
import math

import jax
import jax.numpy as jnp
from jax import lax
from jax.experimental import pallas as pl
from jax.experimental.pallas import tpu as pltpu
from jax.sharding import Mesh
from jax.sharding import PartitionSpec as P

NBLK = 6
ABPO = 4
BF = jnp.bfloat16
F32 = jnp.float32
PAIRS = 16
GROUP = 64
ROWS1 = 136
ROWS2 = 120
ROWS3 = 24
BITS = (0, 1, 3, 2, 4)
VMEM = pltpu.CompilerParams(vmem_limit_bytes=20 * 1024 * 1024)


def dot00(a, b):
    return lax.dot_general(a, b, (((0,), (0,)), ((), ())), preferred_element_type=F32)


def dot10(a, b):
    return lax.dot_general(a, b, (((1,), (0,)), ((), ())), preferred_element_type=F32)


def piece_kernel(
    ints_in, amps_in, coef_in, blocks_in, owners_in, offsets_in,
    out, token, coef, ints, amps, pieces, rounded, blocks, owners, offsets, sems, sends,
):
    pairs_in = [
        (blocks_in, blocks), (owners_in, owners), (offsets_in, offsets), (amps_in, amps)
    ]
    for i in range(4):
        four = slice(4 * i, 4 * i + 4)
        pairs_in += [(ints_in.at[four], ints.at[four]), (coef_in.at[four], coef.at[four])]
    copies = [pltpu.make_async_copy(*pair, sems.at[i]) for i, pair in enumerate(pairs_in)]
    for copy in copies:
        copy.start()
    for copy in copies[:4]:
        copy.wait()
    lane = lax.broadcasted_iota(jnp.int32, (1, 128), 1) % 64
    slice_row = jnp.zeros((1, 128), F32)
    block_row = jnp.zeros((1, 128), F32)
    offset_row = jnp.zeros((1, 128), F32)
    for p in range(PAIRS):
        if p % 4 == 0:
            copies[4 + p // 2].wait()
            copies[5 + p // 2].wait()
        three_index = dot00(amps[p], ints[p]).astype(BF)
        piece = dot00(coef[p], three_index)
        for h in range(2):
            for k in range(2):
                slot = 4 * p + 2 * h + k
                pieces[pl.ds(slot, 128, 64), :] = piece[
                    128 * h : 128 * h + 128, 128 * k : 128 * k + 128
                ]
                here = lane == slot
                slice_row = jnp.where(here, owners[k, p].astype(F32), slice_row)
                block_row = jnp.where(here, blocks[h, p].astype(F32), block_row)
                offset_row = jnp.where(here, offsets[k, p].astype(F32), offset_row)
    sub = lax.broadcasted_iota(jnp.int32, (8, 128), 0)
    labels = jnp.where(sub == 0, slice_row, jnp.where(sub == 1, block_row, offset_row))
    token[...] = labels
    labels = labels.astype(BF)
    copies = []
    for i in range(8):
        eight = slice(8 * i, 8 * i + 8)
        for g in range(8 * i, 8 * i + 8):
            rounded[g, 0:128, :] = pieces[128 * g : 128 * g + 128, :].astype(BF)
            rounded[g, 128:ROWS1, :] = labels
        copies.append(pltpu.make_async_copy(rounded.at[eight], out.at[eight], sends.at[i]))
        copies[-1].start()
    for copy in copies:
        copy.wait()


def virtual_kernel(
    bit, dens_in, coef_in, blocks_in, token,
    mine, other, weighted_rows, coef_rows, virt, dens, coef, blocks, sems,
):
    pairs_in = [(dens_in, dens), (coef_in, coef), (blocks_in, blocks)]
    copies = [pltpu.make_async_copy(*pair, sems.at[i]) for i, pair in enumerate(pairs_in)]
    for copy in copies:
        copy.start()
    weighted_rows[...] = jnp.zeros(weighted_rows.shape, BF)
    coef_rows[...] = jnp.zeros(coef_rows.shape, BF)
    for copy in copies:
        copy.wait()
    for p in range(PAIRS):
        c = coef[p]
        weighted = dot00(dens[p], c).astype(BF)
        for h in range(2):
            at = pl.ds(pl.multiple_of(blocks[h, p] * 128, 128), 128)
            weighted_rows[64 * p : 64 * p + 64, at] = weighted[:, 128 * h : 128 * h + 128]
            coef_rows[64 * p : 64 * p + 64, at] = c[:, 128 * h : 128 * h + 128]
    virt[...] = dot00(coef_rows[...], weighted_rows[...])
    for i in range(16):
        mine[i] = virt[pl.ds(pl.multiple_of(48 * i + 24 * bit[0], 8), 24), :]
        away = virt[pl.ds(pl.multiple_of(48 * i + 24 * (1 - bit[0]), 8), 24), :]
        other[i] = away.astype(BF)


def halve_kernel(bit, mine, got, kept, other, *, after):
    for i in range(kept.shape[0]):
        first = (i // after) * 2 * after + i % after
        keep = first + after * bit[0]
        away = first + after * (1 - bit[0])
        kept[i] = mine[keep] + got[keep].astype(F32)
        other[i] = (mine[away] + got[away].astype(F32)).astype(other.dtype)


def place_kernel(got, mine, other, out, hot, acc):
    lane = lax.broadcasted_iota(jnp.int32, (1, 128), 1)
    cell = lax.broadcasted_iota(jnp.int32, (384, 128), 0)
    for i in range(GROUP // 2):
        first = got[2 * i, 128:136, :].astype(F32)
        second = got[2 * i + 1, 128:136, :].astype(F32)
        both = jnp.where(lane < 64, first, second)
        target = both[0:1] * 24.0 + both[1:2] * 4.0 + both[2:3]
        hot[:, 128 * i : 128 * i + 128] = (cell == target.astype(jnp.int32)).astype(BF)
    data = jnp.concatenate(
        [got[:, 0:64, :].reshape(4096, 128), got[:, 64:128, :].reshape(4096, 128)], 1
    )
    acc[...] = dot10(hot[...], data)
    lanes8 = lax.broadcasted_iota(jnp.int32, (8, 128), 1)
    virt = mine[0] + other[0].astype(F32)
    for z in range(8):
        rows = [acc[48 * z : 48 * z + 48, 0:128], acc[48 * z : 48 * z + 48, 128:256]]
        for i in range(3):
            a, b, c = (
                virt[8 * i : 8 * i + 8, 384 * (z // 4) + 128 * j : 384 * (z // 4) + 128 * j + 128]
                for j in range(3)
            )
            if z % 4 == 0:
                rows.append(a)
            elif z % 4 == 1:
                rows.append(jnp.where(lanes8 < 32, pltpu.roll(a, 32, 1), pltpu.roll(b, 32, 1)))
            elif z % 4 == 2:
                rows.append(jnp.where(lanes8 < 64, pltpu.roll(b, 64, 1), pltpu.roll(c, 64, 1)))
            else:
                rows.append(pltpu.roll(c, 96, 1))
        out[z] = jnp.concatenate(rows, 0).astype(BF)


def column_kernel(place, got, out):
    total = got[0].astype(F32)
    for z in range(1, 8):
        total = total + got[z].astype(F32)
    sub = lax.broadcasted_iota(jnp.int32, (8, 128), 0)
    lane = lax.broadcasted_iota(jnp.int32, (8, 128), 1)
    tiles = []
    for i in range(6):
        a, b = total[8 * i : 8 * i + 8], total[48 + 8 * i : 56 + 8 * i]
        tiles.append(jnp.where(sub < 4, a, pltpu.roll(b, 4, 0)))
        tiles.append(jnp.where(sub < 4, pltpu.roll(a, 4, 0), b))
    column = 2 * place[0]
    virt = [total[96 + 8 * i : 104 + 8 * i] for i in range(3)]
    packed = []
    for shift in (0, 80):
        v0, v1, v2 = (pltpu.roll(v, shift, 1) if shift else v for v in virt)
        packed.append([jnp.where(lane < 64, v0, pltpu.roll(v1, 64, 1)), v2])
    for low in range(2):
        for p in range(32):
            b_first, b_last = (24 * p) // 128, (24 * p + 23) // 128
            tile = tiles[6 * low + b_first]
            if b_last != b_first:
                tile = jnp.where(column >= 24 * p - 128 * b_first, tile, tiles[6 * low + b_last])
            out[2 * p + low] = jnp.concatenate([tile] + packed[low], 0).astype(BF)


def final_kernel(place, got, aux_out, virt_out, *, scale):
    p = place[0]
    for j in range(12):
        tile = got[lax.rem(12 * p + j, 64), 0:8, :].astype(F32) * scale
        for y in range(2):
            for o in range(ABPO):
                aux_out[2 * j + y : 2 * j + y + 1, 128 * o : 128 * o + 128] = tile[
                    4 * y + o : 4 * y + o + 1
                ]
    both = (got[2 * p, 8:24, :].astype(F32) + got[2 * p + 1, 8:24, :].astype(F32)) * scale
    virt_out[0:8, :] = both[0:8, 0:48]
    virt_out[8:16, :] = pltpu.roll(both[0:8], 64, 1)[:, 0:48]
    virt_out[16:24, :] = both[8:16, 0:48]


def in_vmem(x):
    return pltpu.with_memory_space_constraint(x, pltpu.VMEM)


def in_hbm(x):
    return pltpu.with_memory_space_constraint(x, pltpu.HBM)


def call(body, ins, outs, scalars=(), scratch=(), held=(), far=0):
    smem = pl.BlockSpec(memory_space=pltpu.SMEM)
    vmem = pl.BlockSpec(memory_space=pltpu.VMEM)
    hbm = pl.BlockSpec(memory_space=pltpu.HBM)
    return pl.pallas_call(
        body,
        in_specs=[smem] * len(scalars) + [hbm] * len(held) + [vmem] * len(ins),
        out_specs=[hbm] * far + [vmem] * (len(outs) - far),
        out_shape=outs,
        scratch_shapes=scratch,
        compiler_params=VMEM,
    )(*scalars, *map(in_hbm, held), *map(in_vmem, ins))


def on_device(integrals, amplitudes, pno_density, pno_coef, pao_blocks, aux_slice, aux_offset):
    pair = lax.axis_index("pair")
    low = lax.axis_index("low")
    scale = 1.0 / math.sqrt(PAIRS * 32)
    sds = jax.ShapeDtypeStruct
    coef, blocks = jnp.swapaxes(pno_coef, 1, 2), pao_blocks.T
    names = pltpu.SMEM((2, PAIRS), jnp.int32)
    sent, token = call(
        piece_kernel,
        [],
        [pltpu.HBM((GROUP, ROWS1, 128), BF), sds((8, 128), F32)],
        scratch=[
            pltpu.VMEM((PAIRS, 64, 256), BF),
            pltpu.VMEM((PAIRS, 64, 256), BF),
            pltpu.VMEM((PAIRS, 64, 64), BF),
            pltpu.VMEM((8192, 128), F32),
            pltpu.VMEM((GROUP, ROWS1, 128), BF),
            names,
            names,
            names,
            pltpu.SemaphoreType.DMA((12,)),
            pltpu.SemaphoreType.DMA((8,)),
        ],
        held=[jnp.swapaxes(integrals, 1, 2), amplitudes, coef, blocks, aux_slice.T, aux_offset.T],
        far=1,
    )
    got = lax.all_to_all(sent, ("pair", "low"), split_axis=0, concat_axis=0, tiled=True)
    bits = [((pair >> b) & 1).reshape(1) for b in BITS]
    mine, other = call(
        virtual_kernel,
        [token],
        [sds((16, 24, 768), F32), sds((16, 24, 768), BF)],
        [bits[0]],
        [
            pltpu.VMEM((1024, 768), BF),
            pltpu.VMEM((1024, 768), BF),
            pltpu.VMEM((768, 768), F32),
            pltpu.VMEM((PAIRS, 64, 64), BF),
            pltpu.VMEM((PAIRS, 64, 256), BF),
            names,
            pltpu.SemaphoreType.DMA((3,)),
        ],
        held=[pno_density, coef, blocks],
    )
    left = [4, 3, 2, 1]
    for i in range(5):
        other = lax.ppermute(other, "pair", [(q, q ^ (1 << BITS[i])) for q in range(32)])
        if i == 4:
            break
        after = 2 ** sum(b < BITS[i + 1] for b in left)
        left.remove(BITS[i + 1])
        kept = mine.shape[0] // 2
        mine, other = call(
            lambda *refs, after=after: halve_kernel(*refs, after=after),
            [mine, other],
            [sds((kept, 24, 768), F32), sds((kept, 24, 768), BF if kept > 2 else F32)],
            [bits[i + 1]],
        )
    (sent,) = call(
        place_kernel,
        [got, mine, other],
        [sds((8, ROWS2, 128), BF)],
        scratch=[pltpu.VMEM((384, 4096), BF), pltpu.VMEM((384, 256), F32)],
    )
    got = lax.all_to_all(sent, "high", split_axis=0, concat_axis=0, tiled=True)
    (sent,) = call(
        column_kernel,
        [got],
        [sds((GROUP, ROWS3, 128), BF)],
        [(2 * pair + low).reshape(1)],
    )
    got = lax.all_to_all(sent, ("pair", "low"), split_axis=0, concat_axis=0, tiled=True)
    aux, virt = call(
        lambda *refs: final_kernel(*refs, scale=scale),
        [got],
        [sds((24, 512), F32), sds((24, 48), F32)],
        [pair.reshape(1)],
    )
    return aux.T, virt.T


def solution(mesh):
    split = Mesh(mesh.devices.reshape(32, 8, 2), ("pair", "high", "low"))
    every = ("pair", "high", "low")
    in_specs = (P(every, None, None),) * 4 + (P(every, None),) * 3
    out_specs = (P(("high", "low"), "pair"),) * 2
    return jax.shard_map(
        on_device, mesh=split, in_specs=in_specs, out_specs=out_specs, check_vma=False
    )
```

```python
import math

import jax
import jax.numpy as jnp
from jax import lax
from jax.experimental import pallas as pl
from jax.experimental.pallas import tpu as pltpu
from jax.sharding import Mesh
from jax.sharding import PartitionSpec as P

NBLK = 6
ABPO = 4
BF = jnp.bfloat16
F32 = jnp.float32
PAIRS = 16
GROUP = 64
ROWS1 = 168
ROWS2 = 112
ROWS3 = 16
VMEM = pltpu.CompilerParams(vmem_limit_bytes=20 * 1024 * 1024)


def dot00(a, b):
    return lax.dot_general(a, b, (((0,), (0,)), ((), ())), preferred_element_type=F32)


def dot10(a, b):
    return lax.dot_general(a, b, (((1,), (0,)), ((), ())), preferred_element_type=F32)


def virtual_kernel(
    core, dens_in, coef_in, blocks_in, ints_in, amps_in,
    mine, other, coef, ints, amps, acc, dens, blocks, sems,
):
    moves = [(blocks_in, blocks), (coef_in, coef), (dens_in, dens), (ints_in, ints), (amps_in, amps)]
    copies = [pltpu.make_async_copy(*move, sems.at[i]) for i, move in enumerate(moves)]
    for copy in copies:
        copy.start()
    acc[...] = jnp.zeros(acc.shape, F32)
    for copy in copies[:3]:
        copy.wait()
    for p in range(PAIRS):
        c = coef[p]
        weighted = dot00(dens[p], c).astype(BF)
        product = dot00(c, weighted)
        for h in range(2):
            for k in range(2):
                at = blocks[h, p] * 6 + blocks[k, p]
                acc[at] = acc[at] + product[128 * h : 128 * h + 128, 128 * k : 128 * k + 128]
    for i in range(6):
        for j in range(3):
            mine[3 * i + j] = acc[6 * i + j + 3 * core[0]]
            other[3 * i + j] = acc[6 * i + j + 3 - 3 * core[0]].astype(BF)
    for copy in copies[3:]:
        copy.wait()


def piece_kernel(ints, amps, coef, out, pieces):
    for p in range(PAIRS):
        three_index = dot00(amps[p], ints[p]).astype(BF)
        piece = dot00(coef[p], three_index)
        for h in range(2):
            for k in range(2):
                pieces[pl.ds(4 * p + 2 * h + k, 128, 64), :] = piece[
                    128 * h : 128 * h + 128, 128 * k : 128 * k + 128
                ]
    for g in range(GROUP):
        out[g, 0:128, :] = pieces[128 * g : 128 * g + 128, :].astype(BF)


def rest_kernel(blocks, owners, offsets, filled, mine, other, out, rows, sem):
    lane = lax.broadcasted_iota(jnp.int32, (1, 128), 1) % 64
    slice_row = jnp.zeros((1, 128), F32)
    block_row = jnp.zeros((1, 128), F32)
    offset_row = jnp.zeros((1, 128), F32)
    for p in range(PAIRS):
        for h in range(2):
            for k in range(2):
                here = lane == 4 * p + 2 * h + k
                slice_row = jnp.where(here, owners[k, p].astype(F32), slice_row)
                block_row = jnp.where(here, blocks[h, p].astype(F32), block_row)
                offset_row = jnp.where(here, offsets[k, p].astype(F32), offset_row)
    sub = lax.broadcasted_iota(jnp.int32, (8, 128), 0)
    top = sub < 4
    labels = jnp.where(sub == 4, slice_row, jnp.where(sub == 5, block_row, offset_row))
    for i in range(GROUP // 2):
        first, mid, last = (
            [
                mine[3 * (row // 128) + j, row % 128 : row % 128 + 8, :]
                + other[3 * (row // 128) + j, row % 128 : row % 128 + 8, :].astype(F32)
                for j in range(3)
            ]
            for row in (24 * i, 24 * i + 8, 24 * i + 16)
        )
        moved = [pltpu.roll(m, 4, 0) for m in mid]
        even = first + [jnp.where(top, mid[0], moved[1]), jnp.where(top, mid[2], labels)]
        odd = last + [jnp.where(top, moved[0], mid[1]), jnp.where(top, moved[2], labels)]
        rows[2 * i] = jnp.concatenate(even, 0).astype(BF)
        rows[2 * i + 1] = jnp.concatenate(odd, 0).astype(BF)
    copy = pltpu.make_async_copy(rows, out.at[:, 128:ROWS1], sem)
    copy.start()
    copy.wait()


def place_kernel(got, out, hot, acc):
    lane = lax.broadcasted_iota(jnp.int32, (1, 128), 1)
    cell = lax.broadcasted_iota(jnp.int32, (384, 128), 0)
    for i in range(GROUP // 2):
        first = got[2 * i, 160:168, :].astype(F32)
        second = got[2 * i + 1, 160:168, :].astype(F32)
        both = jnp.where(lane < 64, first, second)
        target = both[4:5] * 24.0 + both[5:6] * 4.0 + both[6:7]
        hot[:, 128 * i : 128 * i + 128] = (cell == target.astype(jnp.int32)).astype(BF)
    data = jnp.concatenate(
        [got[:, 0:64, :].reshape(4096, 128), got[:, 64:128, :].reshape(4096, 128)], 1
    )
    acc[...] = dot10(hot[...], data)
    lanes8 = lax.broadcasted_iota(jnp.int32, (8, 128), 1)
    for half in range(2):
        mine = [g for g in range(GROUP) if (g // 2) % 2 == half]
        total = got[mine[0], 128:168, :].astype(F32)
        for g in mine[1:]:
            total = total + got[g, 128:168, :].astype(F32)
        whole = [total[0:8], total[8:16], total[16:24]]
        part = [total[24:32], pltpu.roll(total[24:32], 4, 0), total[32:40]]
        for z in range(4):
            at = 4 * half + z
            rows = [acc[48 * at : 48 * at + 48, 0:128], acc[48 * at : 48 * at + 48, 128:256]]
            for a, b, c in (whole, part):
                if z == 0:
                    rows.append(a)
                elif z == 1:
                    rows.append(
                        jnp.where(lanes8 < 32, pltpu.roll(a, 32, 1), pltpu.roll(b, 32, 1))
                    )
                elif z == 2:
                    rows.append(
                        jnp.where(lanes8 < 64, pltpu.roll(b, 64, 1), pltpu.roll(c, 64, 1))
                    )
                else:
                    rows.append(pltpu.roll(c, 96, 1))
            out[at] = jnp.concatenate(rows, 0).astype(BF)


def column_kernel(place, got, out):
    total = got[0].astype(F32)
    for z in range(1, 8):
        total = total + got[z].astype(F32)
    sub = lax.broadcasted_iota(jnp.int32, (8, 128), 0)
    lane = lax.broadcasted_iota(jnp.int32, (8, 128), 1)
    tiles = []
    for i in range(6):
        a, b = total[8 * i : 8 * i + 8], total[48 + 8 * i : 56 + 8 * i]
        tiles.append(jnp.where(sub < 4, a, pltpu.roll(b, 4, 0)))
        tiles.append(jnp.where(sub < 4, pltpu.roll(a, 4, 0), b))
    column = 2 * place[0]
    whole, part = total[96:104], total[104:112]
    packed = [
        jnp.where(lane < 64, whole, pltpu.roll(part, 64, 1)),
        jnp.where(lane < 64, pltpu.roll(whole, 80, 1), pltpu.roll(part, 16, 1)),
    ]
    for low in range(2):
        for p in range(32):
            b_first, b_last = (24 * p) // 128, (24 * p + 23) // 128
            tile = tiles[6 * low + b_first]
            if b_last != b_first:
                tile = jnp.where(column >= 24 * p - 128 * b_first, tile, tiles[6 * low + b_last])
            out[2 * p + low] = jnp.concatenate([tile, packed[low]], 0).astype(BF)


def final_kernel(place, got, aux_out, virt_out, *, scale):
    p = place[0]
    for j in range(12):
        tile = got[lax.rem(12 * p + j, 64), 0:8, :].astype(F32) * scale
        for y in range(2):
            for o in range(ABPO):
                aux_out[2 * j + y : 2 * j + y + 1, 128 * o : 128 * o + 128] = tile[
                    4 * y + o : 4 * y + o + 1
                ]
    sub = lax.broadcasted_iota(jnp.int32, (8, 128), 0)
    first = got[2 * p, 8:16, :].astype(F32) * scale
    last = got[2 * p + 1, 8:16, :].astype(F32) * scale
    mid = jnp.where(sub < 4, pltpu.roll(first, 64, 1), pltpu.roll(pltpu.roll(last, 64, 1), 4, 0))
    virt_out[0:8, :] = first[:, 0:48]
    virt_out[8:16, :] = mid[:, 0:48]
    virt_out[16:24, :] = last[:, 0:48]


def in_vmem(x):
    return pltpu.with_memory_space_constraint(x, pltpu.VMEM)


def in_hbm(x):
    return pltpu.with_memory_space_constraint(x, pltpu.HBM)


def call(body, ins, outs, scalars=(), scratch=(), held=(), in_place=None):
    smem = pl.BlockSpec(memory_space=pltpu.SMEM)
    vmem = pl.BlockSpec(memory_space=pltpu.VMEM)
    hbm = pl.BlockSpec(memory_space=pltpu.HBM)
    some = pl.BlockSpec(memory_space=pl.ANY)
    lead = [] if in_place is None else [in_place]
    return pl.pallas_call(
        body,
        in_specs=[smem] * len(scalars) + [some] * len(lead) + [hbm] * len(held) + [vmem] * len(ins),
        out_specs=[some if lead else vmem] * len(outs),
        out_shape=outs,
        scratch_shapes=scratch,
        input_output_aliases={len(scalars): 0} if lead else {},
        compiler_params=VMEM,
    )(*scalars, *lead, *map(in_hbm, held), *map(in_vmem, ins))


def on_device(integrals, amplitudes, pno_density, pno_coef, pao_blocks, aux_slice, aux_offset):
    pair = lax.axis_index("pair")
    low = lax.axis_index("low")
    scale = 1.0 / math.sqrt(PAIRS * 32)
    sds = jax.ShapeDtypeStruct
    blocks = pao_blocks.T
    mine, other, coef, ints, amps = call(
        virtual_kernel,
        [],
        [
            sds((18, 128, 128), F32),
            sds((18, 128, 128), BF),
            sds((PAIRS, 64, 256), BF),
            sds((PAIRS, 64, 256), BF),
            sds((PAIRS, 64, 64), BF),
        ],
        [(pair % 2).reshape(1)],
        [
            pltpu.VMEM((36, 128, 128), F32),
            pltpu.VMEM((PAIRS, 64, 64), BF),
            pltpu.SMEM((2, PAIRS), jnp.int32),
            pltpu.SemaphoreType.DMA((5,)),
        ],
        held=[
            pno_density,
            jnp.swapaxes(pno_coef, 1, 2),
            blocks,
            jnp.swapaxes(integrals, 1, 2),
            amplitudes,
        ],
    )
    other = lax.ppermute(other, "pair", [(i, i ^ 1) for i in range(32)])
    (filled,) = call(
        piece_kernel,
        [ints, amps, coef],
        [sds((GROUP, ROWS1, 128), BF)],
        scratch=[pltpu.VMEM((8192, 128), F32)],
    )
    (sent,) = call(
        rest_kernel,
        [mine, other],
        [sds((GROUP, ROWS1, 128), BF)],
        [blocks, aux_slice.T, aux_offset.T],
        [pltpu.VMEM((GROUP, ROWS1 - 128, 128), BF), pltpu.SemaphoreType.DMA(())],
        in_place=filled,
    )
    got = lax.all_to_all(sent, ("pair", "low"), split_axis=0, concat_axis=0, tiled=True)
    (sent,) = call(
        place_kernel,
        [got],
        [sds((8, ROWS2, 128), BF)],
        [],
        [pltpu.VMEM((384, 4096), BF), pltpu.VMEM((384, 256), F32)],
    )
    got = lax.all_to_all(sent, "high", split_axis=0, concat_axis=0, tiled=True)
    (sent,) = call(
        column_kernel,
        [got],
        [sds((GROUP, ROWS3, 128), BF)],
        [(2 * pair + low).reshape(1)],
    )
    got = lax.all_to_all(sent, ("pair", "low"), split_axis=0, concat_axis=0, tiled=True)
    aux, virt = call(
        lambda *refs: final_kernel(*refs, scale=scale),
        [got],
        [sds((24, 512), F32), sds((24, 48), F32)],
        [pair.reshape(1)],
    )
    return aux.T, virt.T


def solution(mesh):
    split = Mesh(mesh.devices.reshape(32, 8, 2), ("pair", "high", "low"))
    every = ("pair", "high", "low")
    in_specs = (P(every, None, None),) * 4 + (P(every, None),) * 3
    out_specs = (P(("high", "low"), "pair"),) * 2
    return jax.shard_map(
        on_device, mesh=split, in_specs=in_specs, out_specs=out_specs, check_vma=False
    )
```

```python
import math

import jax
import jax.numpy as jnp
import numpy as np
from jax import lax
from jax.experimental import pallas as pl
from jax.experimental.pallas import tpu as pltpu
from jax.sharding import Mesh
from jax.sharding import PartitionSpec as P

NBLK = 6
ABPO = 4
BF = jnp.bfloat16
F32 = jnp.float32
PAIRS = 16
GROUP = 64
ROWS1 = 168
MEMBERS = 128


def tables():
    spare = {12: 0, 15: 1, 13: 2, 14: 3}, {0: 1, 14: 2, 1: 0, 15: 3}, {0: 2, 13: 3, 14: 0, 15: 1}
    octets = np.zeros((6, 16), np.int32)
    owner = np.zeros((32, 8), np.int32)
    content = np.full((16, 8), 6, np.int32)
    for half in range(2):
        for b in range(3):
            block, left = 3 * half + b, 3 - b
            others = [t for t in range(4) if t != left]
            for o in range(16):
                p = (64 * block + 4 * o) // 12
                if o in spare[b]:
                    octets[block, o] = 4 * spare[b][o] + left
                else:
                    rank = (64 * block + 4 * o - 12 * p) // 4
                    octets[block, o] = 4 * (p % 4) + others[rank]
                    owner[p] = others + [0, 0, left, half, 0]
                    for t in others:
                        content[4 * (p % 4) + t, p // 4] = block
        special = {
            4: [3, 4, 5, 2, 1, 0, half, 0],
            5: [3, 2, 4, 1, 0, 0, half, 0],
            10: [2, 4, 1, 3, 0, 0, half, 0],
            15: [1, 5, 4, 2, 3, 0, half, 0],
        }
        for p, row in special.items():
            owner[p + 16 * half] = row
            for t in range(1, 4):
                content[4 * (p % 4) + t, (p + 16 * half) // 4] = 3 * half + 3 - t
    return octets, owner, content


OCTETS, OWNER, CONTENT = tables()
ROUND1 = [(a + h, b + h) for h in (0, 16) for a, b in ((4, 5), (5, 15), (10, 4), (15, 10))]
ROUND2 = [(a + h, b + h) for h in (0, 16) for a, b in ((4, 15), (15, 4))]
VMEM = pltpu.CompilerParams(vmem_limit_bytes=20 * 1024 * 1024)


def dot00(a, b):
    return lax.dot_general(a, b, (((0,), (0,)), ((), ())), preferred_element_type=F32)


def dot10(a, b):
    return lax.dot_general(a, b, (((1,), (0,)), ((), ())), preferred_element_type=F32)


def virtual_kernel(
    core, dens_in, coef_in, blocks_in, ints_in, amps_in,
    mine, other, coef, ints, amps, acc, dens, blocks, sems,
):
    moves = [(blocks_in, blocks), (coef_in, coef), (dens_in, dens), (ints_in, ints), (amps_in, amps)]
    copies = [pltpu.make_async_copy(*move, sems.at[i]) for i, move in enumerate(moves)]
    for copy in copies:
        copy.start()
    acc[...] = jnp.zeros(acc.shape, F32)
    for copy in copies[:3]:
        copy.wait()
    for p in range(PAIRS):
        c = coef[p]
        weighted = dot00(dens[p], c).astype(BF)
        product = dot00(c, weighted)
        for h in range(2):
            for k in range(2):
                at = blocks[h, p] * 6 + blocks[k, p]
                acc[at] = acc[at] + product[128 * h : 128 * h + 128, 128 * k : 128 * k + 128]
    for i in range(6):
        for j in range(3):
            mine[3 * i + j] = acc[6 * i + j + 3 * core[0]]
            other[3 * i + j] = acc[6 * i + j + 3 - 3 * core[0]].astype(BF)
    for copy in copies[3:]:
        copy.wait()


def piece_kernel(blocks, octets, ints, amps, coef, out, pieces):
    for p in range(PAIRS):
        three_index = dot00(amps[p], ints[p]).astype(BF)
        piece = dot00(coef[p], three_index)
        for h in range(2):
            block = blocks[h, p]
            for o in range(16):
                start = octets[block, o] * 512 + 4 * p + 2 * h
                for k in range(2):
                    pieces[pl.ds(start + k, 8, 64), :] = piece[
                        128 * h + 8 * o : 128 * h + 8 * o + 8, 128 * k : 128 * k + 128
                    ]
    for g in range(GROUP):
        high, low = g // 8, g % 8
        at = (4 * (low // 2) + high // 2) * 512 + (2 * (high % 2) + low % 2) * 128
        out[g, 0:128, :] = pieces[at : at + 128, :].astype(BF)


def rest_kernel(blocks, owners, offsets, filled, mine, other, out, rows, sem):
    lane = lax.broadcasted_iota(jnp.int32, (1, 128), 1) % 64
    slice_row = jnp.zeros((1, 128), F32)
    block_row = jnp.zeros((1, 128), F32)
    offset_row = jnp.zeros((1, 128), F32)
    for p in range(PAIRS):
        for h in range(2):
            for k in range(2):
                here = lane == 4 * p + 2 * h + k
                slice_row = jnp.where(here, owners[k, p].astype(F32), slice_row)
                block_row = jnp.where(here, blocks[h, p].astype(F32), block_row)
                offset_row = jnp.where(here, offsets[k, p].astype(F32), offset_row)
    sub = lax.broadcasted_iota(jnp.int32, (8, 128), 0)
    top = sub < 4
    labels = jnp.where(sub == 4, slice_row, jnp.where(sub == 5, block_row, offset_row))
    for i in range(GROUP // 2):
        first, mid, last = (
            [
                mine[3 * (row // 128) + j, row % 128 : row % 128 + 8, :]
                + other[3 * (row // 128) + j, row % 128 : row % 128 + 8, :].astype(F32)
                for j in range(3)
            ]
            for row in (24 * i, 24 * i + 8, 24 * i + 16)
        )
        moved = [pltpu.roll(m, 4, 0) for m in mid]
        even = first + [jnp.where(top, mid[0], moved[1]), jnp.where(top, mid[2], labels)]
        odd = last + [jnp.where(top, moved[0], mid[1]), jnp.where(top, moved[2], labels)]
        to = 2 * (4 * (2 * int(OWNER[i, 5]) + int(OWNER[i, 6])) + i % 4)
        rows[to] = jnp.concatenate(even, 0).astype(BF)
        rows[to + 1] = jnp.concatenate(odd, 0).astype(BF)
    copy = pltpu.make_async_copy(rows, out.at[:, 128:ROWS1], sem)
    copy.start()
    copy.wait()


def place_kernel(place, content, got, out, hot, acc, tiles):
    lane = lax.broadcasted_iota(jnp.int32, (1, 128), 1)
    cell = lax.broadcasted_iota(jnp.int32, (384, 128), 0)
    for i in range(GROUP // 2):
        first = got[2 * i, 160:168, :].astype(F32)
        second = got[2 * i + 1, 160:168, :].astype(F32)
        both = jnp.where(lane < 64, first, second)
        target = both[4:5] * 24.0 + both[5:6] * 4.0 + both[6:7]
        hot[:, 128 * i : 128 * i + 128] = (cell == target.astype(jnp.int32)).astype(BF)
    data = jnp.concatenate(
        [got[:, 0:64, :].reshape(4096, 128), got[:, 64:128, :].reshape(4096, 128)], 1
    )
    acc[...] = dot10(hot[...], data)
    top = lax.broadcasted_iota(jnp.int32, (8, 128), 0) < 4
    for z in range(16):
        for i in range(3):
            a = acc[24 * z + 8 * i : 24 * z + 8 * i + 8, 0:128]
            b = acc[24 * z + 8 * i : 24 * z + 8 * i + 8, 128:256]
            tiles[7 * z + 2 * i] = jnp.where(top, a, pltpu.roll(b, 4, 0))
            tiles[7 * z + 2 * i + 1] = jnp.where(top, pltpu.roll(a, 4, 0), b)
    wide = lax.broadcasted_iota(jnp.int32, (8, 128), 1)
    for half in range(2):
        mine = [g for g in range(GROUP) if (g // 2) % 2 == half]
        total = got[mine[0], 128:168, :].astype(F32)
        for g in mine[1:]:
            total = total + got[g, 128:168, :].astype(F32)
        whole = [total[0:8], total[8:16], total[16:24]]
        part = [total[24:32], pltpu.roll(total[24:32], 4, 0), total[32:40]]
        for m in range(8):
            at, off = (48 * m) // 128, (48 * m) % 128
            cut = 128 - off
            ends = []
            for group, base in ((whole, 0), (part, 64)):
                shift = (base - off) % 128
                end = pltpu.roll(group[at], shift, 1) if shift else group[at]
                if cut < 48:
                    beyond = pltpu.roll(group[at + 1], shift, 1) if shift else group[at + 1]
                    end = jnp.where(wide < base + cut, end, beyond)
                ends.append(end)
            tiles[7 * (8 * half + m) + 6] = jnp.where(wide < 64, ends[0], ends[1])
    for q in range(8):
        which = content[place[0], q]
        for z in range(16):
            out[16 * q + z] = tiles[7 * z + which].astype(BF)


def sum_kernel(place, owner, got, sums, first, second, virt_out, *, scale):
    p = place[0]
    for i in range(16):
        total = got[16 * (i // 2) + i % 2].astype(F32)
        for z in range(1, 8):
            total = total + got[16 * (i // 2) + 2 * z + i % 2].astype(F32)
        sums[i] = total * scale
    for j in range(4):
        first[j] = sums[4 * owner[p, 3] + j]
        second[j] = sums[4 * owner[p, 4] + j]
    sub = lax.broadcasted_iota(jnp.int32, (8, 128), 0)
    at = 4 * owner[p, 5] + 2 * owner[p, 6]
    even, odd = sums[at], sums[at + 1]
    mid = jnp.where(sub < 4, pltpu.roll(even, 64, 1), pltpu.roll(pltpu.roll(odd, 64, 1), 4, 0))
    virt_out[0:8, :] = even[:, 0:48]
    virt_out[8:16, :] = mid[:, 0:48]
    virt_out[16:24, :] = odd[:, 0:48]


def final_kernel(place, owner, sums, first, second, aux_out, stack):
    p = place[0]
    stack[0:16] = sums[...]
    stack[16:20] = first[...]
    stack[20:24] = second[...]
    for r in range(3):
        at = 4 * owner[p, r]
        for j in range(4):
            tile = stack[at + j]
            for y in range(2):
                row = 8 * r + 2 * j + y
                for o in range(ABPO):
                    aux_out[row : row + 1, 128 * o : 128 * o + 128] = tile[
                        4 * y + o : 4 * y + o + 1
                    ]


def in_vmem(x):
    return pltpu.with_memory_space_constraint(x, pltpu.VMEM)


def in_hbm(x):
    return pltpu.with_memory_space_constraint(x, pltpu.HBM)


def call(body, ins, outs, scalars=(), scratch=(), held=(), in_place=None):
    smem = pl.BlockSpec(memory_space=pltpu.SMEM)
    vmem = pl.BlockSpec(memory_space=pltpu.VMEM)
    hbm = pl.BlockSpec(memory_space=pltpu.HBM)
    some = pl.BlockSpec(memory_space=pl.ANY)
    lead = [] if in_place is None else [in_place]
    return pl.pallas_call(
        body,
        in_specs=[smem] * len(scalars) + [some] * len(lead) + [hbm] * len(held) + [vmem] * len(ins),
        out_specs=[some if lead else vmem] * len(outs),
        out_shape=outs,
        scratch_shapes=scratch,
        input_output_aliases={len(scalars): 0} if lead else {},
        compiler_params=VMEM,
    )(*scalars, *lead, *map(in_hbm, held), *map(in_vmem, ins))


def on_device(integrals, amplitudes, pno_density, pno_coef, pao_blocks, aux_slice, aux_offset):
    pair_high = lax.axis_index("pair_high")
    pair_low = lax.axis_index("pair_low")
    pair = 4 * pair_high + pair_low
    both = ("pair_high", "pair_low")
    scale = 1.0 / math.sqrt(PAIRS * 32)
    sds = jax.ShapeDtypeStruct
    blocks = pao_blocks.T
    mine, other, coef, ints, amps = call(
        virtual_kernel,
        [],
        [
            sds((18, 128, 128), F32),
            sds((18, 128, 128), BF),
            sds((PAIRS, 64, 256), BF),
            sds((PAIRS, 64, 256), BF),
            sds((PAIRS, 64, 64), BF),
        ],
        [(pair % 2).reshape(1)],
        [
            pltpu.VMEM((36, 128, 128), F32),
            pltpu.VMEM((PAIRS, 64, 64), BF),
            pltpu.SMEM((2, PAIRS), jnp.int32),
            pltpu.SemaphoreType.DMA((5,)),
        ],
        held=[
            pno_density,
            jnp.swapaxes(pno_coef, 1, 2),
            blocks,
            jnp.swapaxes(integrals, 1, 2),
            amplitudes,
        ],
    )
    other = lax.ppermute(other, both, [(i, i ^ 1) for i in range(32)])
    (filled,) = call(
        piece_kernel,
        [ints, amps, coef],
        [sds((GROUP, ROWS1, 128), BF)],
        [blocks, jnp.asarray(OCTETS)],
        scratch=[pltpu.VMEM((8192, 128), F32)],
    )
    (sent,) = call(
        rest_kernel,
        [mine, other],
        [sds((GROUP, ROWS1, 128), BF)],
        [blocks, aux_slice.T, aux_offset.T],
        [pltpu.VMEM((GROUP, ROWS1 - 128, 128), BF), pltpu.SemaphoreType.DMA(())],
        in_place=filled,
    )
    got = lax.all_to_all(sent, (*both, "low"), split_axis=0, concat_axis=0, tiled=True)
    (sent,) = call(
        place_kernel,
        [got],
        [sds((MEMBERS, 8, 128), BF)],
        [(4 * pair_low + pair_high // 2).reshape(1), jnp.asarray(CONTENT)],
        [
            pltpu.VMEM((384, 4096), BF),
            pltpu.VMEM((384, 256), F32),
            pltpu.VMEM((112, 8, 128), F32),
        ],
    )
    axes = ("pair_high", "high", "low")
    got = lax.all_to_all(sent, axes, split_axis=0, concat_axis=0, tiled=True)
    place = [pair.reshape(1), jnp.asarray(OWNER)]
    parcel = sds((4, 8, 128), F32)
    sums, first, second, virt = call(
        lambda *refs: sum_kernel(*refs, scale=scale),
        [got],
        [sds((16, 8, 128), F32), parcel, parcel, sds((24, 48), F32)],
        place,
    )
    first = lax.ppermute(first, both, ROUND1)
    second = lax.ppermute(second, both, ROUND2)
    (aux,) = call(
        final_kernel,
        [sums, first, second],
        [sds((24, 512), F32)],
        place,
        [pltpu.VMEM((24, 8, 128), F32)],
    )
    return aux.T, virt.T


def solution(mesh):
    names = ("pair_high", "pair_low", "high", "low")
    split = Mesh(mesh.devices.reshape(8, 4, 8, 2), names)
    in_specs = (P(names, None, None),) * 4 + (P(names, None),) * 3
    out_specs = (P(("high", "low"), ("pair_high", "pair_low")),) * 2
    return jax.shard_map(
        on_device, mesh=split, in_specs=in_specs, out_specs=out_specs, check_vma=False
    )
```

```python
import math

import jax
import jax.numpy as jnp
from jax import lax
from jax.experimental import pallas as pl
from jax.experimental.pallas import tpu as pltpu
from jax.sharding import Mesh
from jax.sharding import PartitionSpec as P

NBLK = 6
ABPO = 4
BF = jnp.bfloat16
F32 = jnp.float32
PAIRS = 16
GROUP = 64
ROWS1 = 168
ROWS2 = 112
STRIDE = 68


def matching():
    free = [
        [q for q in range(32) if all((64 * b + 2 * q + z) // 12 != p for z in (0, 1) for b in range(6))]
        for p in range(32)
    ]
    chosen = {}

    def place(p, seen):
        for q in free[p]:
            if q not in seen:
                seen.add(q)
                if q not in chosen or place(chosen[q], seen):
                    chosen[q] = p
                    return True
        return False

    assert all(place(p, set()) for p in range(32))
    return [2 * q + z for p in range(32) for q in range(32) if chosen[q] == p for z in (0, 1)]


TAKES = matching()
HOLDER = [TAKES.index(pair) for pair in range(GROUP)]
VMEM = pltpu.CompilerParams(vmem_limit_bytes=20 * 1024 * 1024)


def dot00(a, b):
    return lax.dot_general(a, b, (((0,), (0,)), ((), ())), preferred_element_type=F32)


def dot10(a, b):
    return lax.dot_general(a, b, (((1,), (0,)), ((), ())), preferred_element_type=F32)


def virtual_kernel(
    core, dens_in, coef_in, blocks_in, ints_in, amps_in,
    mine, other, coef, ints, amps, acc, dens, blocks, sems,
):
    moves = [(blocks_in, blocks), (coef_in, coef), (dens_in, dens), (ints_in, ints), (amps_in, amps)]
    copies = [pltpu.make_async_copy(*move, sems.at[i]) for i, move in enumerate(moves)]
    for copy in copies:
        copy.start()
    acc[...] = jnp.zeros(acc.shape, F32)
    for copy in copies[:3]:
        copy.wait()
    for p in range(PAIRS):
        c = coef[p]
        weighted = dot00(dens[p], c).astype(BF)
        product = dot00(c, weighted)
        for h in range(2):
            for k in range(2):
                at = blocks[h, p] * 6 + blocks[k, p]
                acc[at] = acc[at] + product[128 * h : 128 * h + 128, 128 * k : 128 * k + 128]
    for i in range(6):
        for j in range(3):
            mine[3 * i + j] = acc[6 * i + j + 3 * core[0]]
            other[3 * i + j] = acc[6 * i + j + 3 - 3 * core[0]].astype(BF)
    for copy in copies[3:]:
        copy.wait()


def piece_kernel(ints, amps, coef, out, pieces):
    for p in range(PAIRS):
        three_index = dot00(amps[p], ints[p]).astype(BF)
        piece = dot00(coef[p], three_index)
        for h in range(2):
            for k in range(2):
                pieces[pl.ds(4 * p + 2 * h + k, 128, STRIDE), :] = piece[
                    128 * h : 128 * h + 128, 128 * k : 128 * k + 128
                ]
    for g in range(GROUP):
        for y in range(2):
            at = (2 * TAKES[g] + y) * STRIDE
            out[g, 64 * y : 64 * y + 64, :] = pieces[at : at + 64, :].astype(BF)


def rest_kernel(blocks, owners, offsets, filled, mine, other, out, rows, sem):
    lane = lax.broadcasted_iota(jnp.int32, (1, 128), 1) % 64
    slice_row = jnp.zeros((1, 128), F32)
    block_row = jnp.zeros((1, 128), F32)
    offset_row = jnp.zeros((1, 128), F32)
    for p in range(PAIRS):
        for h in range(2):
            for k in range(2):
                here = lane == 4 * p + 2 * h + k
                slice_row = jnp.where(here, owners[k, p].astype(F32), slice_row)
                block_row = jnp.where(here, blocks[h, p].astype(F32), block_row)
                offset_row = jnp.where(here, offsets[k, p].astype(F32), offset_row)
    sub = lax.broadcasted_iota(jnp.int32, (8, 128), 0)
    top = sub < 4
    labels = jnp.where(sub == 4, slice_row, jnp.where(sub == 5, block_row, offset_row))
    for i in range(GROUP // 2):
        first, mid, last = (
            [
                mine[3 * (row // 128) + j, row % 128 : row % 128 + 8, :]
                + other[3 * (row // 128) + j, row % 128 : row % 128 + 8, :].astype(F32)
                for j in range(3)
            ]
            for row in (24 * i, 24 * i + 8, 24 * i + 16)
        )
        moved = [pltpu.roll(m, 4, 0) for m in mid]
        even = first + [jnp.where(top, mid[0], moved[1]), jnp.where(top, mid[2], labels)]
        odd = last + [jnp.where(top, moved[0], mid[1]), jnp.where(top, moved[2], labels)]
        rows[2 * i] = jnp.concatenate(even, 0).astype(BF)
        rows[2 * i + 1] = jnp.concatenate(odd, 0).astype(BF)
    copy = pltpu.make_async_copy(rows, out.at[:, 128:ROWS1], sem)
    copy.start()
    copy.wait()


def place_kernel(got, out, hot, acc):
    lane = lax.broadcasted_iota(jnp.int32, (1, 128), 1)
    cell = lax.broadcasted_iota(jnp.int32, (384, 128), 0)
    for i in range(GROUP // 2):
        first = got[2 * i, 160:168, :].astype(F32)
        second = got[2 * i + 1, 160:168, :].astype(F32)
        both = jnp.where(lane < 64, first, second)
        target = both[4:5] * 24.0 + both[5:6] * 4.0 + both[6:7]
        hot[:, 128 * i : 128 * i + 128] = (cell == target.astype(jnp.int32)).astype(BF)
    data = jnp.concatenate(
        [got[:, 0:64, :].reshape(4096, 128), got[:, 64:128, :].reshape(4096, 128)], 1
    )
    acc[...] = dot10(hot[...], data)
    lanes8 = lax.broadcasted_iota(jnp.int32, (8, 128), 1)
    for half in range(2):
        mine = [g for g in range(GROUP) if (g // 2) % 2 == half]
        total = got[mine[0], 128:168, :].astype(F32)
        for g in mine[1:]:
            total = total + got[g, 128:168, :].astype(F32)
        whole = [total[0:8], total[8:16], total[16:24]]
        part = [total[24:32], pltpu.roll(total[24:32], 4, 0), total[32:40]]
        for z in range(4):
            at = 4 * half + z
            rows = [acc[48 * at : 48 * at + 48, 0:128], acc[48 * at : 48 * at + 48, 128:256]]
            for a, b, c in (whole, part):
                if z == 0:
                    rows.append(a)
                elif z == 1:
                    rows.append(
                        jnp.where(lanes8 < 32, pltpu.roll(a, 32, 1), pltpu.roll(b, 32, 1))
                    )
                elif z == 2:
                    rows.append(
                        jnp.where(lanes8 < 64, pltpu.roll(b, 64, 1), pltpu.roll(c, 64, 1))
                    )
                else:
                    rows.append(pltpu.roll(c, 96, 1))
            out[at] = jnp.concatenate(rows, 0).astype(BF)


def column_kernel(place, takes, got, out):
    total = got[0].astype(F32)
    for z in range(1, 8):
        total = total + got[z].astype(F32)
    sub = lax.broadcasted_iota(jnp.int32, (8, 128), 0)
    lane = lax.broadcasted_iota(jnp.int32, (8, 128), 1)
    tiles = []
    for i in range(6):
        a, b = total[8 * i : 8 * i + 8], total[48 + 8 * i : 56 + 8 * i]
        tiles.append(jnp.where(sub < 4, a, pltpu.roll(b, 4, 0)))
        tiles.append(jnp.where(sub < 4, pltpu.roll(a, 4, 0), b))
    column = 2 * takes[place[0]]
    whole, part = total[96:104], total[104:112]
    packed = [
        jnp.where(lane < 64, whole, pltpu.roll(part, 64, 1)),
        jnp.where(lane < 64, pltpu.roll(whole, 80, 1), pltpu.roll(part, 16, 1)),
    ]
    for low in range(2):
        for p in range(32):
            b_first, b_last = (24 * p) // 128, (24 * p + 23) // 128
            tile = tiles[6 * low + b_first]
            if b_last != b_first:
                tile = jnp.where(column >= 24 * p - 128 * b_first, tile, tiles[6 * low + b_last])
            out[2 * p + low] = tile.astype(BF)
    for low in range(2):
        out[place[0] // 2 * 2 + low] = packed[low].astype(BF)


def final_kernel(place, holder, got, aux_out, virt_out, *, scale):
    p = place[0]
    for j in range(12):
        tile = got[holder[lax.rem(12 * p + j, 64)]].astype(F32) * scale
        for y in range(2):
            for o in range(ABPO):
                aux_out[2 * j + y : 2 * j + y + 1, 128 * o : 128 * o + 128] = tile[
                    4 * y + o : 4 * y + o + 1
                ]
    sub = lax.broadcasted_iota(jnp.int32, (8, 128), 0)
    first = got[2 * p].astype(F32) * scale
    last = got[2 * p + 1].astype(F32) * scale
    mid = jnp.where(sub < 4, pltpu.roll(first, 64, 1), pltpu.roll(pltpu.roll(last, 64, 1), 4, 0))
    virt_out[0:8, :] = first[:, 0:48]
    virt_out[8:16, :] = mid[:, 0:48]
    virt_out[16:24, :] = last[:, 0:48]


def in_vmem(x):
    return pltpu.with_memory_space_constraint(x, pltpu.VMEM)


def in_hbm(x):
    return pltpu.with_memory_space_constraint(x, pltpu.HBM)


def call(body, ins, outs, scalars=(), scratch=(), held=(), in_place=None):
    smem = pl.BlockSpec(memory_space=pltpu.SMEM)
    vmem = pl.BlockSpec(memory_space=pltpu.VMEM)
    hbm = pl.BlockSpec(memory_space=pltpu.HBM)
    some = pl.BlockSpec(memory_space=pl.ANY)
    lead = [] if in_place is None else [in_place]
    return pl.pallas_call(
        body,
        in_specs=[smem] * len(scalars) + [some] * len(lead) + [hbm] * len(held) + [vmem] * len(ins),
        out_specs=[some if lead else vmem] * len(outs),
        out_shape=outs,
        scratch_shapes=scratch,
        input_output_aliases={len(scalars): 0} if lead else {},
        compiler_params=VMEM,
    )(*scalars, *lead, *map(in_hbm, held), *map(in_vmem, ins))


def on_device(integrals, amplitudes, pno_density, pno_coef, pao_blocks, aux_slice, aux_offset):
    pair = lax.axis_index("pair")
    low = lax.axis_index("low")
    scale = 1.0 / math.sqrt(PAIRS * 32)
    sds = jax.ShapeDtypeStruct
    blocks = pao_blocks.T
    mine, other, coef, ints, amps = call(
        virtual_kernel,
        [],
        [
            sds((18, 128, 128), F32),
            sds((18, 128, 128), BF),
            sds((PAIRS, 64, 256), BF),
            sds((PAIRS, 64, 256), BF),
            sds((PAIRS, 64, 64), BF),
        ],
        [(pair % 2).reshape(1)],
        [
            pltpu.VMEM((36, 128, 128), F32),
            pltpu.VMEM((PAIRS, 64, 64), BF),
            pltpu.SMEM((2, PAIRS), jnp.int32),
            pltpu.SemaphoreType.DMA((5,)),
        ],
        held=[
            pno_density,
            jnp.swapaxes(pno_coef, 1, 2),
            blocks,
            jnp.swapaxes(integrals, 1, 2),
            amplitudes,
        ],
    )
    other = lax.ppermute(other, "pair", [(i, i ^ 1) for i in range(32)])
    (filled,) = call(
        piece_kernel,
        [ints, amps, coef],
        [sds((GROUP, ROWS1, 128), BF)],
        scratch=[pltpu.VMEM((128 * STRIDE, 128), F32)],
    )
    (sent,) = call(
        rest_kernel,
        [mine, other],
        [sds((GROUP, ROWS1, 128), BF)],
        [blocks, aux_slice.T, aux_offset.T],
        [pltpu.VMEM((GROUP, ROWS1 - 128, 128), BF), pltpu.SemaphoreType.DMA(())],
        in_place=filled,
    )
    got = lax.all_to_all(sent, ("pair", "low"), split_axis=0, concat_axis=0, tiled=True)
    (sent,) = call(
        place_kernel,
        [got],
        [sds((8, ROWS2, 128), BF)],
        [],
        [pltpu.VMEM((384, 4096), BF), pltpu.VMEM((384, 256), F32)],
    )
    got = lax.all_to_all(sent, "high", split_axis=0, concat_axis=0, tiled=True)
    (sent,) = call(
        column_kernel,
        [got],
        [sds((GROUP, 8, 128), BF)],
        [(2 * pair + low).reshape(1), jnp.array(TAKES, jnp.int32)],
    )
    got = lax.all_to_all(sent, ("pair", "low"), split_axis=0, concat_axis=0, tiled=True)
    aux, virt = call(
        lambda *refs: final_kernel(*refs, scale=scale),
        [got],
        [sds((24, 512), F32), sds((24, 48), F32)],
        [pair.reshape(1), jnp.array(HOLDER, jnp.int32)],
    )
    return aux.T, virt.T


def solution(mesh):
    split = Mesh(mesh.devices.reshape(32, 8, 2), ("pair", "high", "low"))
    every = ("pair", "high", "low")
    in_specs = (P(every, None, None),) * 4 + (P(every, None),) * 3
    out_specs = (P(("high", "low"), "pair"),) * 2
    return jax.shard_map(
        on_device, mesh=split, in_specs=in_specs, out_specs=out_specs, check_vma=False
    )
```

```python
import math

import jax
import jax.numpy as jnp
from jax import lax
from jax.experimental import pallas as pl
from jax.experimental.pallas import tpu as pltpu
from jax.sharding import Mesh
from jax.sharding import PartitionSpec as P

NBLK = 6
ABPO = 4
BF = jnp.bfloat16
F32 = jnp.float32
PAIRS = 16
GROUP = 64
ROWS1 = 168
ROWS2 = 112
STRIDE = 68

VMEM = pltpu.CompilerParams(vmem_limit_bytes=20 * 1024 * 1024)


def taken(g):
    p = g // 2
    return 2 * ((6 * p + 8 + p // 16) % 32) + g % 2


def dot00(a, b):
    return lax.dot_general(a, b, (((0,), (0,)), ((), ())), preferred_element_type=F32)


def dot10(a, b):
    return lax.dot_general(a, b, (((1,), (0,)), ((), ())), preferred_element_type=F32)


def virtual_kernel(
    core, dens_in, coef_in, blocks_in, owners_in, offsets_in, ints_in, amps_in,
    mine, other, coef, ints, amps, labels,
    acc, dens, weighted, blocks, owners, offsets, sems,
):
    moves = [
        (blocks_in, blocks), (coef_in, coef), (dens_in, dens), (owners_in, owners),
        (offsets_in, offsets), (ints_in, ints), (amps_in, amps),
    ]
    copies = [pltpu.make_async_copy(*move, sems.at[i]) for i, move in enumerate(moves)]
    for copy in copies:
        copy.start()
    acc[...] = jnp.zeros(acc.shape, F32)
    for copy in copies[:3]:
        copy.wait()
    for p in range(PAIRS):
        weighted[p] = dot00(dens[p], coef[p]).astype(BF)
    for p in range(PAIRS):
        product = dot00(coef[p], weighted[p])
        for h in range(2):
            for k in range(2):
                at = blocks[h, p] * 6 + blocks[k, p]
                acc[at] = acc[at] + product[128 * h : 128 * h + 128, 128 * k : 128 * k + 128]
    for i in range(6):
        for j in range(3):
            mine[3 * i + j] = acc[6 * i + j + 3 * core[0]]
            other[3 * i + j] = acc[6 * i + j + 3 - 3 * core[0]].astype(BF)
    for copy in copies[3:]:
        copy.wait()
    lane = lax.broadcasted_iota(jnp.int32, (1, 128), 1) % 64
    slice_row = jnp.zeros((1, 128), jnp.int32)
    block_row = jnp.zeros((1, 128), jnp.int32)
    offset_row = jnp.zeros((1, 128), jnp.int32)
    for p in range(PAIRS):
        for h in range(2):
            for k in range(2):
                here = lane == 4 * p + 2 * h + k
                slice_row = jnp.where(here, owners[k, p], slice_row)
                block_row = jnp.where(here, blocks[h, p], block_row)
                offset_row = jnp.where(here, offsets[k, p], offset_row)
    sub = lax.broadcasted_iota(jnp.int32, (8, 128), 0)
    labels[...] = jnp.where(
        sub == 4, slice_row, jnp.where(sub == 5, block_row, offset_row)
    ).astype(F32)


def piece_kernel(ints, amps, coef, out, pieces):
    for p in range(PAIRS):
        three_index = dot00(amps[p], ints[p]).astype(BF)
        piece = dot00(coef[p], three_index)
        for h in range(2):
            for k in range(2):
                pieces[pl.ds(4 * p + 2 * h + k, 128, STRIDE), :] = piece[
                    128 * h : 128 * h + 128, 128 * k : 128 * k + 128
                ]
    for g in range(GROUP):
        for y in range(2):
            at = (2 * taken(g) + y) * STRIDE
            out[g, 64 * y : 64 * y + 64, :] = pieces[at : at + 64, :].astype(BF)


def rest_kernel(filled, mine, other, label_rows, out, rows, sem):
    sub = lax.broadcasted_iota(jnp.int32, (8, 128), 0)
    labels = label_rows[...]
    top = sub < 4
    for i in range(GROUP // 2):
        first, mid, last = (
            [
                mine[3 * (row // 128) + j, row % 128 : row % 128 + 8, :]
                + other[3 * (row // 128) + j, row % 128 : row % 128 + 8, :].astype(F32)
                for j in range(3)
            ]
            for row in (24 * i, 24 * i + 8, 24 * i + 16)
        )
        moved = [pltpu.roll(m, 4, 0) for m in mid]
        even = first + [jnp.where(top, mid[0], moved[1]), jnp.where(top, mid[2], labels)]
        odd = last + [jnp.where(top, moved[0], mid[1]), jnp.where(top, moved[2], labels)]
        rows[2 * i] = jnp.concatenate(even, 0).astype(BF)
        rows[2 * i + 1] = jnp.concatenate(odd, 0).astype(BF)
    copy = pltpu.make_async_copy(rows, out.at[:, 128:ROWS1], sem)
    copy.start()
    copy.wait()


def place_kernel(got, out, hot, acc):
    lane = lax.broadcasted_iota(jnp.int32, (1, 128), 1)
    cell = lax.broadcasted_iota(jnp.int32, (384, 128), 0)
    for i in range(GROUP // 2):
        first = got[2 * i, 160:168, :].astype(F32)
        second = got[2 * i + 1, 160:168, :].astype(F32)
        both = jnp.where(lane < 64, first, second)
        target = both[4:5] * 24.0 + both[5:6] * 4.0 + both[6:7]
        hot[:, 128 * i : 128 * i + 128] = (cell == target.astype(jnp.int32)).astype(BF)
    data = jnp.concatenate(
        [got[:, 0:64, :].reshape(4096, 128), got[:, 64:128, :].reshape(4096, 128)], 1
    )
    acc[...] = dot10(hot[...], data)
    lanes8 = lax.broadcasted_iota(jnp.int32, (8, 128), 1)
    for half in range(2):
        mine = [g for g in range(GROUP) if (g // 2) % 2 == half]
        total = got[mine[0], 128:168, :].astype(F32)
        for g in mine[1:]:
            total = total + got[g, 128:168, :].astype(F32)
        whole = [total[0:8], total[8:16], total[16:24]]
        part = [total[24:32], pltpu.roll(total[24:32], 4, 0), total[32:40]]
        for z in range(4):
            at = 4 * half + z
            rows = [acc[48 * at : 48 * at + 48, 0:128], acc[48 * at : 48 * at + 48, 128:256]]
            for a, b, c in (whole, part):
                if z == 0:
                    rows.append(a)
                elif z == 1:
                    rows.append(
                        jnp.where(lanes8 < 32, pltpu.roll(a, 32, 1), pltpu.roll(b, 32, 1))
                    )
                elif z == 2:
                    rows.append(
                        jnp.where(lanes8 < 64, pltpu.roll(b, 64, 1), pltpu.roll(c, 64, 1))
                    )
                else:
                    rows.append(pltpu.roll(c, 96, 1))
            out[at] = jnp.concatenate(rows, 0).astype(BF)


def column_kernel(place, got, out):
    total = got[0].astype(F32)
    for z in range(1, 8):
        total = total + got[z].astype(F32)
    sub = lax.broadcasted_iota(jnp.int32, (8, 128), 0)
    lane = lax.broadcasted_iota(jnp.int32, (8, 128), 1)
    tiles = []
    for i in range(6):
        a, b = total[8 * i : 8 * i + 8], total[48 + 8 * i : 56 + 8 * i]
        tiles.append(jnp.where(sub < 4, a, pltpu.roll(b, 4, 0)))
        tiles.append(jnp.where(sub < 4, pltpu.roll(a, 4, 0), b))
    p = place[0] >> 1
    column = 4 * ((6 * p + 8 + (p >> 4)) & 31) + 2 * (place[0] & 1)
    own = 2 * p
    whole, part = total[96:104], total[104:112]
    packed = [
        jnp.where(lane < 64, whole, pltpu.roll(part, 64, 1)),
        jnp.where(lane < 64, pltpu.roll(whole, 80, 1), pltpu.roll(part, 16, 1)),
    ]
    for low in range(2):
        for p in range(32):
            b_first, b_last = (24 * p) // 128, (24 * p + 23) // 128
            tile = tiles[6 * low + b_first]
            if b_last != b_first:
                tile = jnp.where(column >= 24 * p - 128 * b_first, tile, tiles[6 * low + b_last])
            out[2 * p + low] = tile.astype(BF)
    for low in range(2):
        out[own + low] = packed[low].astype(BF)


def final_kernel(place, got, aux_out, virt_out, *, scale):
    p = place[0]
    for j in range(12):
        q = (6 * p + j // 2) & 31
        odd = q & 1
        tile = got[32 * odd + 2 * ((11 * (((q - odd) >> 1) + 12)) & 15) + j % 2].astype(F32) * scale
        for y in range(2):
            for o in range(ABPO):
                aux_out[2 * j + y : 2 * j + y + 1, 128 * o : 128 * o + 128] = tile[
                    4 * y + o : 4 * y + o + 1
                ]
    sub = lax.broadcasted_iota(jnp.int32, (8, 128), 0)
    first = got[2 * p].astype(F32) * scale
    last = got[2 * p + 1].astype(F32) * scale
    mid = jnp.where(sub < 4, pltpu.roll(first, 64, 1), pltpu.roll(pltpu.roll(last, 64, 1), 4, 0))
    virt_out[0:8, :] = first[:, 0:48]
    virt_out[8:16, :] = mid[:, 0:48]
    virt_out[16:24, :] = last[:, 0:48]


def in_vmem(x):
    return pltpu.with_memory_space_constraint(x, pltpu.VMEM)


def in_hbm(x):
    return pltpu.with_memory_space_constraint(x, pltpu.HBM)


def call(body, ins, outs, scalars=(), scratch=(), held=(), in_place=None):
    smem = pl.BlockSpec(memory_space=pltpu.SMEM)
    vmem = pl.BlockSpec(memory_space=pltpu.VMEM)
    hbm = pl.BlockSpec(memory_space=pltpu.HBM)
    some = pl.BlockSpec(memory_space=pl.ANY)
    lead = [] if in_place is None else [in_place]
    return pl.pallas_call(
        body,
        in_specs=[smem] * len(scalars) + [some] * len(lead) + [hbm] * len(held) + [vmem] * len(ins),
        out_specs=[some if lead else vmem] * len(outs),
        out_shape=outs,
        scratch_shapes=scratch,
        input_output_aliases={len(scalars): 0} if lead else {},
        compiler_params=VMEM,
    )(*scalars, *lead, *map(in_hbm, held), *map(in_vmem, ins))


def on_device(integrals, amplitudes, pno_density, pno_coef, pao_blocks, aux_slice, aux_offset):
    pair = lax.axis_index("pair")
    low = lax.axis_index("low")
    scale = 1.0 / math.sqrt(PAIRS * 32)
    sds = jax.ShapeDtypeStruct
    names = pltpu.SMEM((2, PAIRS), jnp.int32)
    mine, other, coef, ints, amps, labels = call(
        virtual_kernel,
        [],
        [
            sds((18, 128, 128), F32),
            sds((18, 128, 128), BF),
            sds((PAIRS, 64, 256), BF),
            sds((PAIRS, 64, 256), BF),
            sds((PAIRS, 64, 64), BF),
            sds((8, 128), F32),
        ],
        [(pair % 2).reshape(1)],
        [
            pltpu.VMEM((36, 128, 128), F32),
            pltpu.VMEM((PAIRS, 64, 64), BF),
            pltpu.VMEM((PAIRS, 64, 256), BF),
            names,
            names,
            names,
            pltpu.SemaphoreType.DMA((7,)),
        ],
        held=[
            pno_density,
            jnp.swapaxes(pno_coef, 1, 2),
            pao_blocks.T,
            aux_slice.T,
            aux_offset.T,
            jnp.swapaxes(integrals, 1, 2),
            amplitudes,
        ],
    )
    other = lax.ppermute(other, "pair", [(i, i ^ 1) for i in range(32)])
    (filled,) = call(
        piece_kernel,
        [ints, amps, coef],
        [sds((GROUP, ROWS1, 128), BF)],
        scratch=[pltpu.VMEM((128 * STRIDE, 128), F32)],
    )
    (sent,) = call(
        rest_kernel,
        [mine, other, labels],
        [sds((GROUP, ROWS1, 128), BF)],
        scratch=[pltpu.VMEM((GROUP, ROWS1 - 128, 128), BF), pltpu.SemaphoreType.DMA(())],
        in_place=filled,
    )
    got = lax.all_to_all(sent, ("pair", "low"), split_axis=0, concat_axis=0, tiled=True)
    (sent,) = call(
        place_kernel,
        [got],
        [sds((8, ROWS2, 128), BF)],
        [],
        [pltpu.VMEM((384, 4096), BF), pltpu.VMEM((384, 256), F32)],
    )
    got = lax.all_to_all(sent, "high", split_axis=0, concat_axis=0, tiled=True)
    (sent,) = call(
        column_kernel,
        [got],
        [sds((GROUP, 8, 128), BF)],
        [(2 * pair + low).reshape(1)],
    )
    got = lax.all_to_all(sent, ("pair", "low"), split_axis=0, concat_axis=0, tiled=True)
    aux, virt = call(
        lambda *refs: final_kernel(*refs, scale=scale),
        [got],
        [sds((24, 512), F32), sds((24, 48), F32)],
        [pair.reshape(1)],
    )
    return aux.T, virt.T


def solution(mesh):
    split = Mesh(mesh.devices.reshape(32, 8, 2), ("pair", "high", "low"))
    every = ("pair", "high", "low")
    in_specs = (P(every, None, None),) * 4 + (P(every, None),) * 3
    out_specs = (P(("high", "low"), "pair"),) * 2
    return jax.shard_map(
        on_device, mesh=split, in_specs=in_specs, out_specs=out_specs, check_vma=False
    )
```

```python
import math

import jax
import jax.numpy as jnp
from jax import lax
from jax.experimental import pallas as pl
from jax.experimental.pallas import tpu as pltpu
from jax.sharding import Mesh
from jax.sharding import PartitionSpec as P

NBLK = 6
ABPO = 4
BF = jnp.bfloat16
F32 = jnp.float32
PAIRS = 16
GROUP = 64
ROWS1 = 168
ROWS2 = 112
STRIDE = 68

VMEM = pltpu.CompilerParams(vmem_limit_bytes=20 * 1024 * 1024)


def taken(g):
    p = g // 2
    return 2 * ((6 * p + 8 + p // 16) % 32) + g % 2


def dot00(a, b):
    return lax.dot_general(a, b, (((0,), (0,)), ((), ())), preferred_element_type=F32)


def dot10(a, b):
    return lax.dot_general(a, b, (((1,), (0,)), ((), ())), preferred_element_type=F32)


def virtual_kernel(
    place, dens_in, coef_in, blocks_in, owners_in, offsets_in, ints_in, amps_in,
    acc, other, coef, ints, amps, labels,
    dens, weighted, blocks, owners, offsets, sems,
):
    moves = [
        (blocks_in, blocks), (coef_in, coef), (dens_in, dens), (owners_in, owners),
        (offsets_in, offsets), (ints_in, ints), (amps_in, amps),
    ]
    copies = [pltpu.make_async_copy(*move, sems.at[i]) for i, move in enumerate(moves)]
    for copy in copies:
        copy.start()
    acc[...] = jnp.zeros(acc.shape, F32)
    for copy in copies[:3]:
        copy.wait()
    for p in range(PAIRS):
        weighted[p] = dot00(dens[p], coef[p]).astype(BF)
    for p in range(PAIRS):
        product = dot00(coef[p], weighted[p])
        for h in range(2):
            for k in range(2):
                at = blocks[h, p] * 6 + blocks[k, p]
                acc[at] = acc[at] + product[128 * h : 128 * h + 128, 128 * k : 128 * k + 128]
    core = (place[0] >> 1) & 1
    for i in range(6):
        for j in range(3):
            other[3 * i + j] = acc[6 * i + j + 3 - 3 * core].astype(BF)
    for copy in copies[3:]:
        copy.wait()
    lane = lax.broadcasted_iota(jnp.int32, (1, 128), 1) % 64
    slice_row = jnp.zeros((1, 128), jnp.int32)
    block_row = jnp.zeros((1, 128), jnp.int32)
    offset_row = jnp.zeros((1, 128), jnp.int32)
    for p in range(PAIRS):
        for h in range(2):
            for k in range(2):
                here = lane == 4 * p + 2 * h + k
                slice_row = jnp.where(here, owners[k, p], slice_row)
                block_row = jnp.where(here, blocks[h, p], block_row)
                offset_row = jnp.where(here, offsets[k, p], offset_row)
    sub = lax.broadcasted_iota(jnp.int32, (8, 128), 0)
    labels[...] = jnp.where(
        sub == 4, slice_row, jnp.where(sub == 5, block_row, offset_row)
    ).astype(F32)


def piece_kernel(ints, amps, coef, out, pieces, three_index):
    for p in range(PAIRS):
        three_index[p] = dot00(amps[p], ints[p]).astype(BF)
    for p in range(PAIRS):
        piece = dot00(coef[p], three_index[p])
        for h in range(2):
            for k in range(2):
                pieces[pl.ds(4 * p + 2 * h + k, 128, STRIDE), :] = piece[
                    128 * h : 128 * h + 128, 128 * k : 128 * k + 128
                ]
    for g in range(GROUP):
        for y in range(2):
            at = (2 * taken(g) + y) * STRIDE
            out[g, 64 * y : 64 * y + 64, :] = pieces[at : at + 64, :].astype(BF)


def rest_kernel(place, filled, acc, other, label_rows, out, rows, sem):
    half = 3 * ((place[0] >> 1) & 1)
    sub = lax.broadcasted_iota(jnp.int32, (8, 128), 0)
    labels = label_rows[...]
    top = sub < 4
    for i in range(GROUP // 2):
        first, mid, last = (
            [
                acc[6 * (row // 128) + j + half, row % 128 : row % 128 + 8, :]
                + other[3 * (row // 128) + j, row % 128 : row % 128 + 8, :].astype(F32)
                for j in range(3)
            ]
            for row in (24 * i, 24 * i + 8, 24 * i + 16)
        )
        moved = [pltpu.roll(m, 4, 0) for m in mid]
        even = first + [jnp.where(top, mid[0], moved[1]), jnp.where(top, mid[2], labels)]
        odd = last + [jnp.where(top, moved[0], mid[1]), jnp.where(top, moved[2], labels)]
        rows[2 * i] = jnp.concatenate(even, 0).astype(BF)
        rows[2 * i + 1] = jnp.concatenate(odd, 0).astype(BF)
    copy = pltpu.make_async_copy(rows, out.at[:, 128:ROWS1], sem)
    copy.start()
    copy.wait()


def place_kernel(got, out, hot, acc):
    lane = lax.broadcasted_iota(jnp.int32, (1, 128), 1)
    cell = lax.broadcasted_iota(jnp.int32, (384, 128), 0)
    for i in range(GROUP // 2):
        first = got[2 * i, 160:168, :].astype(F32)
        second = got[2 * i + 1, 160:168, :].astype(F32)
        both = jnp.where(lane < 64, first, second)
        target = both[4:5] * 24.0 + both[5:6] * 4.0 + both[6:7]
        hot[:, 128 * i : 128 * i + 128] = (cell == target.astype(jnp.int32)).astype(BF)
    data = jnp.concatenate(
        [got[:, 0:64, :].reshape(4096, 128), got[:, 64:128, :].reshape(4096, 128)], 1
    )
    acc[...] = dot10(hot[...], data)
    lanes8 = lax.broadcasted_iota(jnp.int32, (8, 128), 1)
    for half in range(2):
        mine = [g for g in range(GROUP) if (g // 2) % 2 == half]
        total = got[mine[0], 128:168, :].astype(F32)
        for g in mine[1:]:
            total = total + got[g, 128:168, :].astype(F32)
        whole = [total[0:8], total[8:16], total[16:24]]
        part = [total[24:32], pltpu.roll(total[24:32], 4, 0), total[32:40]]
        for z in range(4):
            at = 4 * half + z
            rows = [acc[48 * at : 48 * at + 48, 0:128], acc[48 * at : 48 * at + 48, 128:256]]
            for a, b, c in (whole, part):
                if z == 0:
                    rows.append(a)
                elif z == 1:
                    rows.append(
                        jnp.where(lanes8 < 32, pltpu.roll(a, 32, 1), pltpu.roll(b, 32, 1))
                    )
                elif z == 2:
                    rows.append(
                        jnp.where(lanes8 < 64, pltpu.roll(b, 64, 1), pltpu.roll(c, 64, 1))
                    )
                else:
                    rows.append(pltpu.roll(c, 96, 1))
            out[at] = jnp.concatenate(rows, 0).astype(BF)


def column_kernel(place, got, out):
    total = got[0].astype(F32)
    for z in range(1, 8):
        total = total + got[z].astype(F32)
    sub = lax.broadcasted_iota(jnp.int32, (8, 128), 0)
    lane = lax.broadcasted_iota(jnp.int32, (8, 128), 1)
    tiles = []
    for i in range(6):
        a, b = total[8 * i : 8 * i + 8], total[48 + 8 * i : 56 + 8 * i]
        tiles.append(jnp.where(sub < 4, a, pltpu.roll(b, 4, 0)))
        tiles.append(jnp.where(sub < 4, pltpu.roll(a, 4, 0), b))
    p = place[0] >> 1
    column = 4 * ((6 * p + 8 + (p >> 4)) & 31) + 2 * (place[0] & 1)
    own = 2 * p
    whole, part = total[96:104], total[104:112]
    packed = [
        jnp.where(lane < 64, whole, pltpu.roll(part, 64, 1)),
        jnp.where(lane < 64, pltpu.roll(whole, 80, 1), pltpu.roll(part, 16, 1)),
    ]
    for low in range(2):
        for p in range(32):
            b_first, b_last = (24 * p) // 128, (24 * p + 23) // 128
            tile = tiles[6 * low + b_first]
            if b_last != b_first:
                tile = jnp.where(column >= 24 * p - 128 * b_first, tile, tiles[6 * low + b_last])
            out[2 * p + low] = tile.astype(BF)
    for low in range(2):
        out[own + low] = packed[low].astype(BF)


def final_kernel(place, got, aux_out, virt_out, *, scale):
    p = place[0] >> 1
    for j in range(12):
        q = (6 * p + j // 2) & 31
        odd = q & 1
        tile = got[32 * odd + 2 * ((11 * (((q - odd) >> 1) + 12)) & 15) + j % 2].astype(F32) * scale
        for y in range(2):
            for o in range(ABPO):
                aux_out[2 * j + y : 2 * j + y + 1, 128 * o : 128 * o + 128] = tile[
                    4 * y + o : 4 * y + o + 1
                ]
    sub = lax.broadcasted_iota(jnp.int32, (8, 128), 0)
    first = got[2 * p].astype(F32) * scale
    last = got[2 * p + 1].astype(F32) * scale
    mid = jnp.where(sub < 4, pltpu.roll(first, 64, 1), pltpu.roll(pltpu.roll(last, 64, 1), 4, 0))
    virt_out[0:8, :] = first[:, 0:48]
    virt_out[8:16, :] = mid[:, 0:48]
    virt_out[16:24, :] = last[:, 0:48]


def in_vmem(x):
    return pltpu.with_memory_space_constraint(x, pltpu.VMEM)


def in_hbm(x):
    return pltpu.with_memory_space_constraint(x, pltpu.HBM)


def call(body, ins, outs, scalars=(), scratch=(), held=(), in_place=None):
    smem = pl.BlockSpec(memory_space=pltpu.SMEM)
    vmem = pl.BlockSpec(memory_space=pltpu.VMEM)
    hbm = pl.BlockSpec(memory_space=pltpu.HBM)
    some = pl.BlockSpec(memory_space=pl.ANY)
    lead = [] if in_place is None else [in_place]
    return pl.pallas_call(
        body,
        in_specs=[smem] * len(scalars) + [some] * len(lead) + [hbm] * len(held) + [vmem] * len(ins),
        out_specs=[some if lead else vmem] * len(outs),
        out_shape=outs,
        scratch_shapes=scratch,
        input_output_aliases={len(scalars): 0} if lead else {},
        compiler_params=VMEM,
    )(*scalars, *lead, *map(in_hbm, held), *map(in_vmem, ins))


def on_device(integrals, amplitudes, pno_density, pno_coef, pao_blocks, aux_slice, aux_offset):
    place = [(2 * lax.axis_index("pair") + lax.axis_index("low")).reshape(1)]
    scale = 1.0 / math.sqrt(PAIRS * 32)
    sds = jax.ShapeDtypeStruct
    names = pltpu.SMEM((2, PAIRS), jnp.int32)
    acc, other, coef, ints, amps, labels = call(
        virtual_kernel,
        [],
        [
            sds((36, 128, 128), F32),
            sds((18, 128, 128), BF),
            sds((PAIRS, 64, 256), BF),
            sds((PAIRS, 64, 256), BF),
            sds((PAIRS, 64, 64), BF),
            sds((8, 128), F32),
        ],
        place,
        [
            pltpu.VMEM((PAIRS, 64, 64), BF),
            pltpu.VMEM((PAIRS, 64, 256), BF),
            names,
            names,
            names,
            pltpu.SemaphoreType.DMA((7,)),
        ],
        held=[
            pno_density,
            jnp.swapaxes(pno_coef, 1, 2),
            pao_blocks.T,
            aux_slice.T,
            aux_offset.T,
            jnp.swapaxes(integrals, 1, 2),
            amplitudes,
        ],
    )
    other = lax.ppermute(other, "pair", [(i, i ^ 1) for i in range(32)])
    (filled,) = call(
        piece_kernel,
        [ints, amps, coef],
        [sds((GROUP, ROWS1, 128), BF)],
        scratch=[pltpu.VMEM((128 * STRIDE, 128), F32), pltpu.VMEM((PAIRS, 64, 256), BF)],
    )
    (sent,) = call(
        rest_kernel,
        [acc, other, labels],
        [sds((GROUP, ROWS1, 128), BF)],
        place,
        scratch=[pltpu.VMEM((GROUP, ROWS1 - 128, 128), BF), pltpu.SemaphoreType.DMA(())],
        in_place=filled,
    )
    got = lax.all_to_all(sent, ("pair", "low"), split_axis=0, concat_axis=0, tiled=True)
    (sent,) = call(
        place_kernel,
        [got],
        [sds((8, ROWS2, 128), BF)],
        [],
        [pltpu.VMEM((384, 4096), BF), pltpu.VMEM((384, 256), F32)],
    )
    got = lax.all_to_all(sent, "high", split_axis=0, concat_axis=0, tiled=True)
    (sent,) = call(
        column_kernel,
        [got],
        [sds((GROUP, 8, 128), BF)],
        place,
    )
    got = lax.all_to_all(sent, ("pair", "low"), split_axis=0, concat_axis=0, tiled=True)
    aux, virt = call(
        lambda *refs: final_kernel(*refs, scale=scale),
        [got],
        [sds((24, 512), F32), sds((24, 48), F32)],
        place,
    )
    return aux.T, virt.T


def solution(mesh):
    split = Mesh(mesh.devices.reshape(32, 8, 2), ("pair", "high", "low"))
    every = ("pair", "high", "low")
    in_specs = (P(every, None, None),) * 4 + (P(every, None),) * 3
    out_specs = (P(("high", "low"), "pair"),) * 2
    return jax.shard_map(
        on_device, mesh=split, in_specs=in_specs, out_specs=out_specs, check_vma=False
    )
```

```python
import math

import jax
import jax.numpy as jnp
from jax import lax
from jax.experimental import pallas as pl
from jax.experimental.pallas import tpu as pltpu
from jax.sharding import Mesh
from jax.sharding import PartitionSpec as P

NBLK = 6
ABPO = 4
BF = jnp.bfloat16
F32 = jnp.float32
PAIRS = 16
GROUP = 64
ROWS1 = 168
ROWS2 = 112
STRIDE = 68

VMEM = pltpu.CompilerParams(vmem_limit_bytes=20 * 1024 * 1024)


def seat(g):
    p = g // 2
    return 8 * (p % 8) + 2 * (p // 8) + g % 2


def taken(g):
    p = g // 2
    return 2 * ((6 * p + 8 + p // 16) % 32) + g % 2


def dot00(a, b):
    return lax.dot_general(a, b, (((0,), (0,)), ((), ())), preferred_element_type=F32)


def dot10(a, b):
    return lax.dot_general(a, b, (((1,), (0,)), ((), ())), preferred_element_type=F32)


def virtual_kernel(
    place, dens_in, coef_in, blocks_in, owners_in, offsets_in, ints_in, amps_in,
    acc, other, coef, ints, amps, labels,
    dens, weighted, blocks, owners, offsets, sems,
):
    moves = [
        (blocks_in, blocks), (coef_in, coef), (dens_in, dens), (owners_in, owners),
        (offsets_in, offsets), (ints_in, ints), (amps_in, amps),
    ]
    copies = [pltpu.make_async_copy(*move, sems.at[i]) for i, move in enumerate(moves)]
    for copy in copies:
        copy.start()
    acc[...] = jnp.zeros(acc.shape, F32)
    for copy in copies[:3]:
        copy.wait()
    for p in range(PAIRS):
        weighted[p] = dot00(dens[p], coef[p]).astype(BF)
    for p in range(PAIRS):
        product = dot00(coef[p], weighted[p])
        for h in range(2):
            for k in range(2):
                at = blocks[h, p] * 6 + blocks[k, p]
                acc[at] = acc[at] + product[128 * h : 128 * h + 128, 128 * k : 128 * k + 128]
    core = (place[0] >> 1) & 1
    for i in range(6):
        for j in range(3):
            other[3 * i + j] = acc[6 * i + j + 3 - 3 * core].astype(BF)
    for copy in copies[3:]:
        copy.wait()
    lane = lax.broadcasted_iota(jnp.int32, (1, 128), 1) % 64
    slice_row = jnp.zeros((1, 128), jnp.int32)
    block_row = jnp.zeros((1, 128), jnp.int32)
    offset_row = jnp.zeros((1, 128), jnp.int32)
    for p in range(PAIRS):
        for h in range(2):
            for k in range(2):
                here = lane == 4 * p + 2 * h + k
                slice_row = jnp.where(here, owners[k, p], slice_row)
                block_row = jnp.where(here, blocks[h, p], block_row)
                offset_row = jnp.where(here, offsets[k, p], offset_row)
    sub = lax.broadcasted_iota(jnp.int32, (8, 128), 0)
    labels[...] = jnp.where(
        sub == 4, slice_row, jnp.where(sub == 5, block_row, offset_row)
    ).astype(F32)


def piece_kernel(ints, amps, coef, out, pieces, three_index):
    for p in range(PAIRS):
        three_index[p] = dot00(amps[p], ints[p]).astype(BF)
    for p in range(PAIRS):
        piece = dot00(coef[p], three_index[p])
        for h in range(2):
            for k in range(2):
                pieces[pl.ds(4 * p + 2 * h + k, 128, STRIDE), :] = piece[
                    128 * h : 128 * h + 128, 128 * k : 128 * k + 128
                ]
    for g in range(GROUP):
        for y in range(2):
            at = (2 * taken(g) + y) * STRIDE
            out[seat(g), 64 * y : 64 * y + 64, :] = pieces[at : at + 64, :].astype(BF)


def rest_kernel(place, filled, acc, other, label_rows, out, rows, sem):
    half = 3 * ((place[0] >> 1) & 1)
    sub = lax.broadcasted_iota(jnp.int32, (8, 128), 0)
    labels = label_rows[...]
    top = sub < 4
    for i in range(GROUP // 2):
        first, mid, last = (
            [
                acc[6 * (row // 128) + j + half, row % 128 : row % 128 + 8, :]
                + other[3 * (row // 128) + j, row % 128 : row % 128 + 8, :].astype(F32)
                for j in range(3)
            ]
            for row in (24 * i, 24 * i + 8, 24 * i + 16)
        )
        moved = [pltpu.roll(m, 4, 0) for m in mid]
        even = first + [jnp.where(top, mid[0], moved[1]), jnp.where(top, mid[2], labels)]
        odd = last + [jnp.where(top, moved[0], mid[1]), jnp.where(top, moved[2], labels)]
        rows[seat(2 * i)] = jnp.concatenate(even, 0).astype(BF)
        rows[seat(2 * i + 1)] = jnp.concatenate(odd, 0).astype(BF)
    copy = pltpu.make_async_copy(rows, out.at[:, 128:ROWS1], sem)
    copy.start()
    copy.wait()


def place_kernel(got, out, hot, acc):
    lane = lax.broadcasted_iota(jnp.int32, (1, 128), 1)
    cell = lax.broadcasted_iota(jnp.int32, (384, 128), 0)
    for i in range(GROUP // 2):
        first = got[2 * i, 160:168, :].astype(F32)
        second = got[2 * i + 1, 160:168, :].astype(F32)
        both = jnp.where(lane < 64, first, second)
        target = both[4:5] * 24.0 + both[5:6] * 4.0 + both[6:7]
        hot[:, 128 * i : 128 * i + 128] = (cell == target.astype(jnp.int32)).astype(BF)
    data = jnp.concatenate(
        [got[:, 0:64, :].reshape(4096, 128), got[:, 64:128, :].reshape(4096, 128)], 1
    )
    acc[...] = dot10(hot[...], data)
    lanes8 = lax.broadcasted_iota(jnp.int32, (8, 128), 1)
    for half in range(2):
        mine = [g for g in range(GROUP) if (g // 8) % 2 == half]
        total = got[mine[0], 128:168, :].astype(F32)
        for g in mine[1:]:
            total = total + got[g, 128:168, :].astype(F32)
        whole = [total[0:8], total[8:16], total[16:24]]
        part = [total[24:32], pltpu.roll(total[24:32], 4, 0), total[32:40]]
        for z in range(4):
            at = 4 * half + z
            rows = [acc[48 * at : 48 * at + 48, 0:128], acc[48 * at : 48 * at + 48, 128:256]]
            for a, b, c in (whole, part):
                if z == 0:
                    rows.append(a)
                elif z == 1:
                    rows.append(
                        jnp.where(lanes8 < 32, pltpu.roll(a, 32, 1), pltpu.roll(b, 32, 1))
                    )
                elif z == 2:
                    rows.append(
                        jnp.where(lanes8 < 64, pltpu.roll(b, 64, 1), pltpu.roll(c, 64, 1))
                    )
                else:
                    rows.append(pltpu.roll(c, 96, 1))
            out[at] = jnp.concatenate(rows, 0).astype(BF)


def column_kernel(place, got, out):
    total = got[0].astype(F32)
    for z in range(1, 8):
        total = total + got[z].astype(F32)
    sub = lax.broadcasted_iota(jnp.int32, (8, 128), 0)
    lane = lax.broadcasted_iota(jnp.int32, (8, 128), 1)
    tiles = []
    for i in range(6):
        a, b = total[8 * i : 8 * i + 8], total[48 + 8 * i : 56 + 8 * i]
        tiles.append(jnp.where(sub < 4, a, pltpu.roll(b, 4, 0)))
        tiles.append(jnp.where(sub < 4, pltpu.roll(a, 4, 0), b))
    p = place[0] >> 1
    column = 4 * ((6 * p + 8 + (p >> 4)) & 31) + 2 * (place[0] & 1)
    own = 8 * (p & 7) + 2 * (p >> 3)
    whole, part = total[96:104], total[104:112]
    packed = [
        jnp.where(lane < 64, whole, pltpu.roll(part, 64, 1)),
        jnp.where(lane < 64, pltpu.roll(whole, 80, 1), pltpu.roll(part, 16, 1)),
    ]
    for low in range(2):
        for p in range(32):
            b_first, b_last = (24 * p) // 128, (24 * p + 23) // 128
            tile = tiles[6 * low + b_first]
            if b_last != b_first:
                tile = jnp.where(column >= 24 * p - 128 * b_first, tile, tiles[6 * low + b_last])
            out[seat(2 * p + low)] = tile.astype(BF)
    for low in range(2):
        out[own + low] = packed[low].astype(BF)


def final_kernel(place, got, aux_out, virt_out, *, scale):
    p = place[0] >> 1
    for j in range(12):
        q = (6 * p + j // 2) & 31
        odd = q & 1
        holder = 16 * odd + ((11 * (((q - odd) >> 1) + 12)) & 15)
        tile = got[8 * (holder & 7) + 2 * (holder >> 3) + j % 2].astype(F32) * scale
        for y in range(2):
            for o in range(ABPO):
                aux_out[2 * j + y : 2 * j + y + 1, 128 * o : 128 * o + 128] = tile[
                    4 * y + o : 4 * y + o + 1
                ]
    sub = lax.broadcasted_iota(jnp.int32, (8, 128), 0)
    own = 8 * (p & 7) + 2 * (p >> 3)
    first = got[own].astype(F32) * scale
    last = got[own + 1].astype(F32) * scale
    mid = jnp.where(sub < 4, pltpu.roll(first, 64, 1), pltpu.roll(pltpu.roll(last, 64, 1), 4, 0))
    virt_out[0:8, :] = first[:, 0:48]
    virt_out[8:16, :] = mid[:, 0:48]
    virt_out[16:24, :] = last[:, 0:48]


def in_vmem(x):
    return pltpu.with_memory_space_constraint(x, pltpu.VMEM)


def in_hbm(x):
    return pltpu.with_memory_space_constraint(x, pltpu.HBM)


def call(body, ins, outs, scalars=(), scratch=(), held=(), in_place=None):
    smem = pl.BlockSpec(memory_space=pltpu.SMEM)
    vmem = pl.BlockSpec(memory_space=pltpu.VMEM)
    hbm = pl.BlockSpec(memory_space=pltpu.HBM)
    some = pl.BlockSpec(memory_space=pl.ANY)
    lead = [] if in_place is None else [in_place]
    return pl.pallas_call(
        body,
        in_specs=[smem] * len(scalars) + [some] * len(lead) + [hbm] * len(held) + [vmem] * len(ins),
        out_specs=[some if lead else vmem] * len(outs),
        out_shape=outs,
        scratch_shapes=scratch,
        input_output_aliases={len(scalars): 0} if lead else {},
        compiler_params=VMEM,
    )(*scalars, *lead, *map(in_hbm, held), *map(in_vmem, ins))


def on_device(integrals, amplitudes, pno_density, pno_coef, pao_blocks, aux_slice, aux_offset):
    pair = 8 * lax.axis_index("y") + lax.axis_index("x")
    place = [(2 * pair + lax.axis_index("low")).reshape(1)]
    scale = 1.0 / math.sqrt(PAIRS * 32)
    sds = jax.ShapeDtypeStruct
    names = pltpu.SMEM((2, PAIRS), jnp.int32)
    acc, other, coef, ints, amps, labels = call(
        virtual_kernel,
        [],
        [
            sds((36, 128, 128), F32),
            sds((18, 128, 128), BF),
            sds((PAIRS, 64, 256), BF),
            sds((PAIRS, 64, 256), BF),
            sds((PAIRS, 64, 64), BF),
            sds((8, 128), F32),
        ],
        place,
        [
            pltpu.VMEM((PAIRS, 64, 64), BF),
            pltpu.VMEM((PAIRS, 64, 256), BF),
            names,
            names,
            names,
            pltpu.SemaphoreType.DMA((7,)),
        ],
        held=[
            pno_density,
            jnp.swapaxes(pno_coef, 1, 2),
            pao_blocks.T,
            aux_slice.T,
            aux_offset.T,
            jnp.swapaxes(integrals, 1, 2),
            amplitudes,
        ],
    )
    other = lax.ppermute(other, ("y", "x"), [(i, i ^ 1) for i in range(32)])
    (filled,) = call(
        piece_kernel,
        [ints, amps, coef],
        [sds((GROUP, ROWS1, 128), BF)],
        scratch=[pltpu.VMEM((128 * STRIDE, 128), F32), pltpu.VMEM((PAIRS, 64, 256), BF)],
    )
    (sent,) = call(
        rest_kernel,
        [acc, other, labels],
        [sds((GROUP, ROWS1, 128), BF)],
        place,
        scratch=[pltpu.VMEM((GROUP, ROWS1 - 128, 128), BF), pltpu.SemaphoreType.DMA(())],
        in_place=filled,
    )
    got = lax.all_to_all(sent, ("x", "y", "low"), split_axis=0, concat_axis=0, tiled=True)
    (sent,) = call(
        place_kernel,
        [got],
        [sds((8, ROWS2, 128), BF)],
        [],
        [pltpu.VMEM((384, 4096), BF), pltpu.VMEM((384, 256), F32)],
    )
    got = lax.all_to_all(sent, "high", split_axis=0, concat_axis=0, tiled=True)
    (sent,) = call(
        column_kernel,
        [got],
        [sds((GROUP, 8, 128), BF)],
        place,
    )
    got = lax.all_to_all(sent, ("x", "y", "low"), split_axis=0, concat_axis=0, tiled=True)
    aux, virt = call(
        lambda *refs: final_kernel(*refs, scale=scale),
        [got],
        [sds((24, 512), F32), sds((24, 48), F32)],
        place,
    )
    return aux.T, virt.T


def solution(mesh):
    every = ("y", "x", "high", "low")
    split = Mesh(mesh.devices.reshape(4, 8, 8, 2), every)
    in_specs = (P(every, None, None),) * 4 + (P(every, None),) * 3
    out_specs = (P(("high", "low"), ("y", "x")),) * 2
    return jax.shard_map(
        on_device, mesh=split, in_specs=in_specs, out_specs=out_specs, check_vma=False
    )
```

```python
import math

import jax
import jax.numpy as jnp
from jax import lax
from jax.experimental import pallas as pl
from jax.experimental.pallas import tpu as pltpu
from jax.sharding import Mesh
from jax.sharding import PartitionSpec as P

NBLK = 6
ABPO = 4
BF = jnp.bfloat16
F32 = jnp.float32
PAIRS = 16
GROUP = 64
ROWS1 = 168
ROWS2 = 112
STRIDE = 68

VMEM = pltpu.CompilerParams(vmem_limit_bytes=20 * 1024 * 1024)


def seat(g):
    p = g // 2
    return 8 * (p % 8) + 2 * (p // 8) + g % 2


def taken(g):
    p = g // 2
    return 2 * ((6 * p + 8 + p // 16) % 32) + g % 2


def dot00(a, b):
    return lax.dot_general(a, b, (((0,), (0,)), ((), ())), preferred_element_type=F32)


def dot10(a, b):
    return lax.dot_general(a, b, (((1,), (0,)), ((), ())), preferred_element_type=F32)


def virtual_kernel(
    place, dens_in, coef_in, blocks_in, owners_in, offsets_in, ints_in, amps_in,
    acc, other, coef, ints, amps, labels,
    dens, weighted, blocks, owners, offsets, sems,
):
    moves = [
        (blocks_in, blocks), (coef_in, coef), (dens_in, dens), (owners_in, owners),
        (offsets_in, offsets), (ints_in, ints), (amps_in, amps),
    ]
    copies = [pltpu.make_async_copy(*move, sems.at[i]) for i, move in enumerate(moves)]
    for copy in copies:
        copy.start()
    acc[...] = jnp.zeros(acc.shape, F32)
    for copy in copies[:3]:
        copy.wait()
    for p in range(PAIRS):
        weighted[p] = dot00(dens[p], coef[p]).astype(BF)
    for p in range(PAIRS):
        product = dot00(coef[p], weighted[p])
        for h in range(2):
            for k in range(2):
                at = blocks[h, p] * 6 + blocks[k, p]
                acc[at] = acc[at] + product[128 * h : 128 * h + 128, 128 * k : 128 * k + 128]
    core = (place[0] >> 1) & 1
    for i in range(6):
        for j in range(3):
            other[3 * i + j] = acc[6 * i + j + 3 - 3 * core].astype(BF)
    for copy in copies[3:]:
        copy.wait()
    lane = lax.broadcasted_iota(jnp.int32, (1, 128), 1) % 64
    slice_row = jnp.zeros((1, 128), jnp.int32)
    block_row = jnp.zeros((1, 128), jnp.int32)
    offset_row = jnp.zeros((1, 128), jnp.int32)
    for p in range(PAIRS):
        for h in range(2):
            for k in range(2):
                here = lane == 4 * p + 2 * h + k
                slice_row = jnp.where(here, owners[k, p], slice_row)
                block_row = jnp.where(here, blocks[h, p], block_row)
                offset_row = jnp.where(here, offsets[k, p], offset_row)
    sub = lax.broadcasted_iota(jnp.int32, (8, 128), 0)
    labels[...] = jnp.where(
        sub == 4, slice_row, jnp.where(sub == 5, block_row, offset_row)
    ).astype(F32)


def piece_kernel(ints, amps, coef, out, pieces, three_index):
    for p in range(PAIRS):
        three_index[p] = dot00(amps[p], ints[p]).astype(BF)
    for p in range(PAIRS):
        piece = dot00(coef[p], three_index[p])
        for h in range(2):
            for k in range(2):
                pieces[pl.ds(4 * p + 2 * h + k, 128, STRIDE), :] = piece[
                    128 * h : 128 * h + 128, 128 * k : 128 * k + 128
                ]
    for g in range(GROUP):
        for y in range(2):
            at = (2 * taken(g) + y) * STRIDE
            out[seat(g), 64 * y : 64 * y + 64, :] = pieces[at : at + 64, :].astype(BF)


def rest_kernel(place, filled, acc, other, label_rows, out, rows, sem):
    half = 3 * ((place[0] >> 1) & 1)
    sub = lax.broadcasted_iota(jnp.int32, (8, 128), 0)
    labels = label_rows[...]
    top = sub < 4
    for i in range(GROUP // 2):
        first, mid, last = (
            [
                acc[6 * (row // 128) + j + half, row % 128 : row % 128 + 8, :]
                + other[3 * (row // 128) + j, row % 128 : row % 128 + 8, :].astype(F32)
                for j in range(3)
            ]
            for row in (24 * i, 24 * i + 8, 24 * i + 16)
        )
        moved = [pltpu.roll(m, 4, 0) for m in mid]
        even = first + [jnp.where(top, mid[0], moved[1]), jnp.where(top, mid[2], labels)]
        odd = last + [jnp.where(top, moved[0], mid[1]), jnp.where(top, moved[2], labels)]
        rows[seat(2 * i)] = jnp.concatenate(even, 0).astype(BF)
        rows[seat(2 * i + 1)] = jnp.concatenate(odd, 0).astype(BF)
    copy = pltpu.make_async_copy(rows, out.at[:, 128:ROWS1], sem)
    copy.start()
    copy.wait()


def place_kernel(got, out, acc):
    lane = lax.broadcasted_iota(jnp.int32, (1, 128), 1)
    cell = lax.broadcasted_iota(jnp.int32, (384, 128), 0)

    def hot(i):
        first = got[2 * i, 160:168, :].astype(F32)
        second = got[2 * i + 1, 160:168, :].astype(F32)
        both = jnp.where(lane < 64, first, second)
        target = both[4:5] * 24.0 + both[5:6] * 4.0 + both[6:7]
        return (cell == target.astype(jnp.int32)).astype(BF)

    for q in range(8):
        eight = slice(8 * q, 8 * q + 8)
        rows = jnp.concatenate([hot(i) for i in range(4 * q, 4 * q + 4)], 1)
        data = jnp.concatenate(
            [got[eight, 0:64, :].reshape(512, 128), got[eight, 64:128, :].reshape(512, 128)], 1
        )
        part = dot10(rows, data)
        acc[...] = part if q == 0 else acc[...] + part
    lanes8 = lax.broadcasted_iota(jnp.int32, (8, 128), 1)
    for half in range(2):
        mine = [g for g in range(GROUP) if (g // 8) % 2 == half]
        total = got[mine[0], 128:168, :].astype(F32)
        for g in mine[1:]:
            total = total + got[g, 128:168, :].astype(F32)
        whole = [total[0:8], total[8:16], total[16:24]]
        part = [total[24:32], pltpu.roll(total[24:32], 4, 0), total[32:40]]
        for z in range(4):
            at = 4 * half + z
            rows = [acc[48 * at : 48 * at + 48, 0:128], acc[48 * at : 48 * at + 48, 128:256]]
            for a, b, c in (whole, part):
                if z == 0:
                    rows.append(a)
                elif z == 1:
                    rows.append(
                        jnp.where(lanes8 < 32, pltpu.roll(a, 32, 1), pltpu.roll(b, 32, 1))
                    )
                elif z == 2:
                    rows.append(
                        jnp.where(lanes8 < 64, pltpu.roll(b, 64, 1), pltpu.roll(c, 64, 1))
                    )
                else:
                    rows.append(pltpu.roll(c, 96, 1))
            out[at] = jnp.concatenate(rows, 0).astype(BF)


def column_kernel(place, got, out):
    total = got[0].astype(F32)
    for z in range(1, 8):
        total = total + got[z].astype(F32)
    sub = lax.broadcasted_iota(jnp.int32, (8, 128), 0)
    lane = lax.broadcasted_iota(jnp.int32, (8, 128), 1)
    tiles = []
    for i in range(6):
        a, b = total[8 * i : 8 * i + 8], total[48 + 8 * i : 56 + 8 * i]
        tiles.append(jnp.where(sub < 4, a, pltpu.roll(b, 4, 0)))
        tiles.append(jnp.where(sub < 4, pltpu.roll(a, 4, 0), b))
    p = place[0] >> 1
    column = 4 * ((6 * p + 8 + (p >> 4)) & 31) + 2 * (place[0] & 1)
    own = 8 * (p & 7) + 2 * (p >> 3)
    whole, part = total[96:104], total[104:112]
    packed = [
        jnp.where(lane < 64, whole, pltpu.roll(part, 64, 1)),
        jnp.where(lane < 64, pltpu.roll(whole, 80, 1), pltpu.roll(part, 16, 1)),
    ]
    for low in range(2):
        for p in range(32):
            b_first, b_last = (24 * p) // 128, (24 * p + 23) // 128
            tile = tiles[6 * low + b_first]
            if b_last != b_first:
                tile = jnp.where(column >= 24 * p - 128 * b_first, tile, tiles[6 * low + b_last])
            out[seat(2 * p + low)] = tile.astype(BF)
    for low in range(2):
        out[own + low] = packed[low].astype(BF)


def final_kernel(place, got, aux_out, virt_out, *, scale):
    p = place[0] >> 1
    for j in range(12):
        q = (6 * p + j // 2) & 31
        odd = q & 1
        holder = 16 * odd + ((11 * (((q - odd) >> 1) + 12)) & 15)
        tile = got[8 * (holder & 7) + 2 * (holder >> 3) + j % 2].astype(F32) * scale
        for y in range(2):
            for o in range(ABPO):
                aux_out[2 * j + y : 2 * j + y + 1, 128 * o : 128 * o + 128] = tile[
                    4 * y + o : 4 * y + o + 1
                ]
    sub = lax.broadcasted_iota(jnp.int32, (8, 128), 0)
    own = 8 * (p & 7) + 2 * (p >> 3)
    first = got[own].astype(F32) * scale
    last = got[own + 1].astype(F32) * scale
    mid = jnp.where(sub < 4, pltpu.roll(first, 64, 1), pltpu.roll(pltpu.roll(last, 64, 1), 4, 0))
    virt_out[0:8, :] = first[:, 0:48]
    virt_out[8:16, :] = mid[:, 0:48]
    virt_out[16:24, :] = last[:, 0:48]


def in_vmem(x):
    return pltpu.with_memory_space_constraint(x, pltpu.VMEM)


def in_hbm(x):
    return pltpu.with_memory_space_constraint(x, pltpu.HBM)


def call(body, ins, outs, scalars=(), scratch=(), held=(), in_place=None):
    smem = pl.BlockSpec(memory_space=pltpu.SMEM)
    vmem = pl.BlockSpec(memory_space=pltpu.VMEM)
    hbm = pl.BlockSpec(memory_space=pltpu.HBM)
    some = pl.BlockSpec(memory_space=pl.ANY)
    lead = [] if in_place is None else [in_place]
    return pl.pallas_call(
        body,
        in_specs=[smem] * len(scalars) + [some] * len(lead) + [hbm] * len(held) + [vmem] * len(ins),
        out_specs=[some if lead else vmem] * len(outs),
        out_shape=outs,
        scratch_shapes=scratch,
        input_output_aliases={len(scalars): 0} if lead else {},
        compiler_params=VMEM,
    )(*scalars, *lead, *map(in_hbm, held), *map(in_vmem, ins))


def on_device(integrals, amplitudes, pno_density, pno_coef, pao_blocks, aux_slice, aux_offset):
    pair = 8 * lax.axis_index("y") + lax.axis_index("x")
    place = [(2 * pair + lax.axis_index("low")).reshape(1)]
    scale = 1.0 / math.sqrt(PAIRS * 32)
    sds = jax.ShapeDtypeStruct
    names = pltpu.SMEM((2, PAIRS), jnp.int32)
    acc, other, coef, ints, amps, labels = call(
        virtual_kernel,
        [],
        [
            sds((36, 128, 128), F32),
            sds((18, 128, 128), BF),
            sds((PAIRS, 64, 256), BF),
            sds((PAIRS, 64, 256), BF),
            sds((PAIRS, 64, 64), BF),
            sds((8, 128), F32),
        ],
        place,
        [
            pltpu.VMEM((PAIRS, 64, 64), BF),
            pltpu.VMEM((PAIRS, 64, 256), BF),
            names,
            names,
            names,
            pltpu.SemaphoreType.DMA((7,)),
        ],
        held=[
            pno_density,
            jnp.swapaxes(pno_coef, 1, 2),
            pao_blocks.T,
            aux_slice.T,
            aux_offset.T,
            jnp.swapaxes(integrals, 1, 2),
            amplitudes,
        ],
    )
    other = lax.ppermute(other, ("y", "x"), [(i, i ^ 1) for i in range(32)])
    (filled,) = call(
        piece_kernel,
        [ints, amps, coef],
        [sds((GROUP, ROWS1, 128), BF)],
        scratch=[pltpu.VMEM((128 * STRIDE, 128), F32), pltpu.VMEM((PAIRS, 64, 256), BF)],
    )
    (sent,) = call(
        rest_kernel,
        [acc, other, labels],
        [sds((GROUP, ROWS1, 128), BF)],
        place,
        scratch=[pltpu.VMEM((GROUP, ROWS1 - 128, 128), BF), pltpu.SemaphoreType.DMA(())],
        in_place=filled,
    )
    got = lax.all_to_all(sent, ("x", "y", "low"), split_axis=0, concat_axis=0, tiled=True)
    (sent,) = call(
        place_kernel,
        [got],
        [sds((8, ROWS2, 128), BF)],
        [],
        scratch=[pltpu.VMEM((384, 256), F32)],
    )
    got = lax.all_to_all(sent, "high", split_axis=0, concat_axis=0, tiled=True)
    (sent,) = call(
        column_kernel,
        [got],
        [sds((GROUP, 8, 128), BF)],
        place,
    )
    got = lax.all_to_all(sent, ("x", "y", "low"), split_axis=0, concat_axis=0, tiled=True)
    aux, virt = call(
        lambda *refs: final_kernel(*refs, scale=scale),
        [got],
        [sds((24, 512), F32), sds((24, 48), F32)],
        place,
    )
    return aux.T, virt.T


def solution(mesh):
    every = ("y", "x", "high", "low")
    split = Mesh(mesh.devices.reshape(4, 8, 8, 2), every)
    in_specs = (P(every, None, None),) * 4 + (P(every, None),) * 3
    out_specs = (P(("high", "low"), ("y", "x")),) * 2
    return jax.shard_map(
        on_device, mesh=split, in_specs=in_specs, out_specs=out_specs, check_vma=False
    )
```

```python
import math

import jax
import jax.numpy as jnp
from jax import lax
from jax.experimental import pallas as pl
from jax.experimental.pallas import tpu as pltpu
from jax.sharding import Mesh
from jax.sharding import PartitionSpec as P

NBLK = 6
ABPO = 4
BF = jnp.bfloat16
F32 = jnp.float32
PAIRS = 16
GROUP = 64
ROWS1 = 168
ROWS2 = 112
STRIDE = 68

VMEM = pltpu.CompilerParams(vmem_limit_bytes=20 * 1024 * 1024)


def seat(g):
    p = g // 2
    return 8 * (p % 8) + 2 * (p // 8) + g % 2


def taken(g):
    p = g // 2
    return 2 * ((6 * p + 8 + p // 16) % 32) + g % 2


def dot00(a, b):
    return lax.dot_general(a, b, (((0,), (0,)), ((), ())), preferred_element_type=F32)


def dot10(a, b):
    return lax.dot_general(a, b, (((1,), (0,)), ((), ())), preferred_element_type=F32)


def virtual_kernel(
    place, dens_in, coef_in, blocks_in, ints_in, amps_in,
    acc, other, coef, ints, amps, dens, weighted, blocks, sems,
):
    moves = [(blocks_in, blocks), (coef_in, coef), (dens_in, dens), (ints_in, ints), (amps_in, amps)]
    copies = [pltpu.make_async_copy(*move, sems.at[i]) for i, move in enumerate(moves)]
    for copy in copies[:3]:
        copy.start()
    acc[...] = jnp.zeros(acc.shape, F32)
    for copy in copies[:3]:
        copy.wait()
    for copy in copies[3:]:
        copy.start()
    for p in range(PAIRS):
        weighted[p] = dot00(dens[p], coef[p]).astype(BF)
    for p in range(PAIRS):
        product = dot00(coef[p], weighted[p])
        for h in range(2):
            for k in range(2):
                at = blocks[h, p] * 6 + blocks[k, p]
                acc[at] = acc[at] + product[128 * h : 128 * h + 128, 128 * k : 128 * k + 128]
    core = (place[0] >> 1) & 1
    for i in range(6):
        for j in range(3):
            other[3 * i + j] = acc[6 * i + j + 3 - 3 * core].astype(BF)
    for copy in copies[3:]:
        copy.wait()


def piece_kernel(
    blocks_in, owners_in, offsets_in, ints, amps, coef,
    out, labels, pieces, three_index, blocks, owners, offsets, sems,
):
    moves = [(blocks_in, blocks), (owners_in, owners), (offsets_in, offsets)]
    copies = [pltpu.make_async_copy(*move, sems.at[i]) for i, move in enumerate(moves)]
    for copy in copies:
        copy.start()
    for p in range(PAIRS):
        three_index[p] = dot00(amps[p], ints[p]).astype(BF)
    for copy in copies:
        copy.wait()
    lane = lax.broadcasted_iota(jnp.int32, (1, 128), 1) % 64
    slice_row = jnp.zeros((1, 128), jnp.int32)
    block_row = jnp.zeros((1, 128), jnp.int32)
    offset_row = jnp.zeros((1, 128), jnp.int32)
    for p in range(PAIRS):
        piece = dot00(coef[p], three_index[p])
        for h in range(2):
            for k in range(2):
                slot = 4 * p + 2 * h + k
                pieces[pl.ds(slot, 128, STRIDE), :] = piece[
                    128 * h : 128 * h + 128, 128 * k : 128 * k + 128
                ]
                here = lane == slot
                slice_row = jnp.where(here, owners[k, p], slice_row)
                block_row = jnp.where(here, blocks[h, p], block_row)
                offset_row = jnp.where(here, offsets[k, p], offset_row)
    sub = lax.broadcasted_iota(jnp.int32, (8, 128), 0)
    labels[...] = jnp.where(
        sub == 4, slice_row, jnp.where(sub == 5, block_row, offset_row)
    ).astype(F32)
    for g in range(GROUP):
        for y in range(2):
            at = (2 * taken(g) + y) * STRIDE
            out[seat(g), 64 * y : 64 * y + 64, :] = pieces[at : at + 64, :].astype(BF)


def rest_kernel(place, filled, acc, other, label_rows, out, rows, sem):
    half = 3 * ((place[0] >> 1) & 1)
    sub = lax.broadcasted_iota(jnp.int32, (8, 128), 0)
    labels = label_rows[...]
    top = sub < 4
    for i in range(GROUP // 2):
        first, mid, last = (
            [
                acc[6 * (row // 128) + j + half, row % 128 : row % 128 + 8, :]
                + other[3 * (row // 128) + j, row % 128 : row % 128 + 8, :].astype(F32)
                for j in range(3)
            ]
            for row in (24 * i, 24 * i + 8, 24 * i + 16)
        )
        moved = [pltpu.roll(m, 4, 0) for m in mid]
        even = first + [jnp.where(top, mid[0], moved[1]), jnp.where(top, mid[2], labels)]
        odd = last + [jnp.where(top, moved[0], mid[1]), jnp.where(top, moved[2], labels)]
        rows[seat(2 * i)] = jnp.concatenate(even, 0).astype(BF)
        rows[seat(2 * i + 1)] = jnp.concatenate(odd, 0).astype(BF)
    copy = pltpu.make_async_copy(rows, out.at[:, 128:ROWS1], sem)
    copy.start()
    copy.wait()


def place_kernel(got, out, acc):
    lane = lax.broadcasted_iota(jnp.int32, (1, 128), 1)
    cell = lax.broadcasted_iota(jnp.int32, (384, 128), 0)

    def hot(i):
        first = got[2 * i, 160:168, :].astype(F32)
        second = got[2 * i + 1, 160:168, :].astype(F32)
        both = jnp.where(lane < 64, first, second)
        target = both[4:5] * 24.0 + both[5:6] * 4.0 + both[6:7]
        return (cell == target.astype(jnp.int32)).astype(BF)

    for q in range(8):
        eight = slice(8 * q, 8 * q + 8)
        rows = jnp.concatenate([hot(i) for i in range(4 * q, 4 * q + 4)], 1)
        data = jnp.concatenate(
            [got[eight, 0:64, :].reshape(512, 128), got[eight, 64:128, :].reshape(512, 128)], 1
        )
        part = dot10(rows, data)
        acc[...] = part if q == 0 else acc[...] + part
    lanes8 = lax.broadcasted_iota(jnp.int32, (8, 128), 1)
    for half in range(2):
        mine = [g for g in range(GROUP) if (g // 8) % 2 == half]
        total = got[mine[0], 128:168, :].astype(F32)
        for g in mine[1:]:
            total = total + got[g, 128:168, :].astype(F32)
        whole = [total[0:8], total[8:16], total[16:24]]
        part = [total[24:32], pltpu.roll(total[24:32], 4, 0), total[32:40]]
        for z in range(4):
            at = 4 * half + z
            rows = [acc[48 * at : 48 * at + 48, 0:128], acc[48 * at : 48 * at + 48, 128:256]]
            for a, b, c in (whole, part):
                if z == 0:
                    rows.append(a)
                elif z == 1:
                    rows.append(
                        jnp.where(lanes8 < 32, pltpu.roll(a, 32, 1), pltpu.roll(b, 32, 1))
                    )
                elif z == 2:
                    rows.append(
                        jnp.where(lanes8 < 64, pltpu.roll(b, 64, 1), pltpu.roll(c, 64, 1))
                    )
                else:
                    rows.append(pltpu.roll(c, 96, 1))
            out[at] = jnp.concatenate(rows, 0).astype(BF)


def column_kernel(place, got, out):
    total = got[0].astype(F32)
    for z in range(1, 8):
        total = total + got[z].astype(F32)
    sub = lax.broadcasted_iota(jnp.int32, (8, 128), 0)
    lane = lax.broadcasted_iota(jnp.int32, (8, 128), 1)
    tiles = []
    for i in range(6):
        a, b = total[8 * i : 8 * i + 8], total[48 + 8 * i : 56 + 8 * i]
        tiles.append(jnp.where(sub < 4, a, pltpu.roll(b, 4, 0)))
        tiles.append(jnp.where(sub < 4, pltpu.roll(a, 4, 0), b))
    p = place[0] >> 1
    column = 4 * ((6 * p + 8 + (p >> 4)) & 31) + 2 * (place[0] & 1)
    own = 8 * (p & 7) + 2 * (p >> 3)
    whole, part = total[96:104], total[104:112]
    packed = [
        jnp.where(lane < 64, whole, pltpu.roll(part, 64, 1)),
        jnp.where(lane < 64, pltpu.roll(whole, 80, 1), pltpu.roll(part, 16, 1)),
    ]
    for low in range(2):
        for p in range(32):
            b_first, b_last = (24 * p) // 128, (24 * p + 23) // 128
            tile = tiles[6 * low + b_first]
            if b_last != b_first:
                tile = jnp.where(column >= 24 * p - 128 * b_first, tile, tiles[6 * low + b_last])
            out[seat(2 * p + low)] = tile.astype(BF)
    for low in range(2):
        out[own + low] = packed[low].astype(BF)


def final_kernel(place, got, aux_out, virt_out, *, scale):
    p = place[0] >> 1
    for j in range(12):
        q = (6 * p + j // 2) & 31
        odd = q & 1
        holder = 16 * odd + ((11 * (((q - odd) >> 1) + 12)) & 15)
        tile = got[8 * (holder & 7) + 2 * (holder >> 3) + j % 2].astype(F32) * scale
        for y in range(2):
            for o in range(ABPO):
                aux_out[2 * j + y : 2 * j + y + 1, 128 * o : 128 * o + 128] = tile[
                    4 * y + o : 4 * y + o + 1
                ]
    sub = lax.broadcasted_iota(jnp.int32, (8, 128), 0)
    own = 8 * (p & 7) + 2 * (p >> 3)
    first = got[own].astype(F32) * scale
    last = got[own + 1].astype(F32) * scale
    mid = jnp.where(sub < 4, pltpu.roll(first, 64, 1), pltpu.roll(pltpu.roll(last, 64, 1), 4, 0))
    virt_out[0:8, :] = first[:, 0:48]
    virt_out[8:16, :] = mid[:, 0:48]
    virt_out[16:24, :] = last[:, 0:48]


def in_vmem(x):
    return pltpu.with_memory_space_constraint(x, pltpu.VMEM)


def in_hbm(x):
    return pltpu.with_memory_space_constraint(x, pltpu.HBM)


def call(body, ins, outs, scalars=(), scratch=(), held=(), in_place=None):
    smem = pl.BlockSpec(memory_space=pltpu.SMEM)
    vmem = pl.BlockSpec(memory_space=pltpu.VMEM)
    hbm = pl.BlockSpec(memory_space=pltpu.HBM)
    some = pl.BlockSpec(memory_space=pl.ANY)
    lead = [] if in_place is None else [in_place]
    return pl.pallas_call(
        body,
        in_specs=[smem] * len(scalars) + [some] * len(lead) + [hbm] * len(held) + [vmem] * len(ins),
        out_specs=[some if lead else vmem] * len(outs),
        out_shape=outs,
        scratch_shapes=scratch,
        input_output_aliases={len(scalars): 0} if lead else {},
        compiler_params=VMEM,
    )(*scalars, *lead, *map(in_hbm, held), *map(in_vmem, ins))


def on_device(integrals, amplitudes, pno_density, pno_coef, pao_blocks, aux_slice, aux_offset):
    pair = 8 * lax.axis_index("y") + lax.axis_index("x")
    place = [(2 * pair + lax.axis_index("low")).reshape(1)]
    scale = 1.0 / math.sqrt(PAIRS * 32)
    sds = jax.ShapeDtypeStruct
    names = pltpu.SMEM((2, PAIRS), jnp.int32)
    acc, other, coef, ints, amps = call(
        virtual_kernel,
        [],
        [
            sds((36, 128, 128), F32),
            sds((18, 128, 128), BF),
            sds((PAIRS, 64, 256), BF),
            sds((PAIRS, 64, 256), BF),
            sds((PAIRS, 64, 64), BF),
        ],
        place,
        [
            pltpu.VMEM((PAIRS, 64, 64), BF),
            pltpu.VMEM((PAIRS, 64, 256), BF),
            names,
            pltpu.SemaphoreType.DMA((5,)),
        ],
        held=[
            pno_density,
            jnp.swapaxes(pno_coef, 1, 2),
            pao_blocks.T,
            jnp.swapaxes(integrals, 1, 2),
            amplitudes,
        ],
    )
    other = lax.ppermute(other, ("y", "x"), [(i, i ^ 1) for i in range(32)])
    filled, labels = call(
        piece_kernel,
        [ints, amps, coef],
        [sds((GROUP, ROWS1, 128), BF), sds((8, 128), F32)],
        scratch=[
            pltpu.VMEM((128 * STRIDE, 128), F32),
            pltpu.VMEM((PAIRS, 64, 256), BF),
            names,
            names,
            names,
            pltpu.SemaphoreType.DMA((3,)),
        ],
        held=[pao_blocks.T, aux_slice.T, aux_offset.T],
    )
    (sent,) = call(
        rest_kernel,
        [acc, other, labels],
        [sds((GROUP, ROWS1, 128), BF)],
        place,
        scratch=[pltpu.VMEM((GROUP, ROWS1 - 128, 128), BF), pltpu.SemaphoreType.DMA(())],
        in_place=filled,
    )
    got = lax.all_to_all(sent, ("x", "y", "low"), split_axis=0, concat_axis=0, tiled=True)
    (sent,) = call(
        place_kernel,
        [got],
        [sds((8, ROWS2, 128), BF)],
        [],
        scratch=[pltpu.VMEM((384, 256), F32)],
    )
    got = lax.all_to_all(sent, "high", split_axis=0, concat_axis=0, tiled=True)
    (sent,) = call(
        column_kernel,
        [got],
        [sds((GROUP, 8, 128), BF)],
        place,
    )
    got = lax.all_to_all(sent, ("x", "y", "low"), split_axis=0, concat_axis=0, tiled=True)
    aux, virt = call(
        lambda *refs: final_kernel(*refs, scale=scale),
        [got],
        [sds((24, 512), F32), sds((24, 48), F32)],
        place,
    )
    return aux.T, virt.T


def solution(mesh):
    every = ("y", "x", "high", "low")
    split = Mesh(mesh.devices.reshape(4, 8, 8, 2), every)
    in_specs = (P(every, None, None),) * 4 + (P(every, None),) * 3
    out_specs = (P(("high", "low"), ("y", "x")),) * 2
    return jax.shard_map(
        on_device, mesh=split, in_specs=in_specs, out_specs=out_specs, check_vma=False
    )
```

```python
import math

import jax
import jax.numpy as jnp
from jax import lax
from jax.experimental import pallas as pl
from jax.experimental.pallas import tpu as pltpu
from jax.sharding import Mesh
from jax.sharding import PartitionSpec as P

NBLK = 6
ABPO = 4
BF = jnp.bfloat16
F32 = jnp.float32
PAIRS = 16
GROUP = 64
ROWS1 = 168
ROWS2 = 112
STRIDE = 68

VMEM = pltpu.CompilerParams(vmem_limit_bytes=20 * 1024 * 1024)


def seat(g):
    p = g // 2
    return 8 * (p % 8) + 2 * (p // 8) + g % 2


def taken(g):
    p = g // 2
    return 2 * ((6 * p + 8 + p // 16) % 32) + g % 2


def dot00(a, b):
    return lax.dot_general(a, b, (((0,), (0,)), ((), ())), preferred_element_type=F32)


def dot10(a, b):
    return lax.dot_general(a, b, (((1,), (0,)), ((), ())), preferred_element_type=F32)


def virtual_kernel(
    place, dens_in, coef_in, blocks_in, owners_in, offsets_in, ints_in, amps_in,
    acc, other, coef, ints, amps, labels,
    dens, weighted, blocks, owners, offsets, sems,
):
    moves = [
        (coef_in, coef), (dens_in, dens), (blocks_in, blocks), (owners_in, owners),
        (offsets_in, offsets), (ints_in, ints), (amps_in, amps),
    ]
    copies = [pltpu.make_async_copy(*move, sems.at[i]) for i, move in enumerate(moves)]
    for copy in copies:
        copy.start()
    acc[...] = jnp.zeros(acc.shape, F32)
    for copy in copies[:3]:
        copy.wait()
    for p in range(PAIRS):
        weighted[p] = dot00(dens[p], coef[p]).astype(BF)
    for p in range(PAIRS):
        product = dot00(coef[p], weighted[p])
        for h in range(2):
            for k in range(2):
                at = blocks[h, p] * 6 + blocks[k, p]
                acc[at] = acc[at] + product[128 * h : 128 * h + 128, 128 * k : 128 * k + 128]
    core = (place[0] >> 1) & 1
    for i in range(6):
        for j in range(3):
            other[3 * i + j] = acc[6 * i + j + 3 - 3 * core].astype(BF)
    for copy in copies[3:]:
        copy.wait()
    lane = lax.broadcasted_iota(jnp.int32, (1, 128), 1) % 64
    slice_row = jnp.zeros((1, 128), jnp.int32)
    block_row = jnp.zeros((1, 128), jnp.int32)
    offset_row = jnp.zeros((1, 128), jnp.int32)
    for p in range(PAIRS):
        for h in range(2):
            for k in range(2):
                here = lane == 4 * p + 2 * h + k
                slice_row = jnp.where(here, owners[k, p], slice_row)
                block_row = jnp.where(here, blocks[h, p], block_row)
                offset_row = jnp.where(here, offsets[k, p], offset_row)
    sub = lax.broadcasted_iota(jnp.int32, (8, 128), 0)
    labels[...] = jnp.where(
        sub == 4, slice_row, jnp.where(sub == 5, block_row, offset_row)
    ).astype(F32)


def piece_kernel(ints, amps, coef, out, pieces, three_index):
    for p in range(PAIRS):
        three_index[p] = dot00(amps[p], ints[p]).astype(BF)
    for p in range(PAIRS):
        piece = dot00(coef[p], three_index[p])
        for h in range(2):
            for k in range(2):
                pieces[pl.ds(4 * p + 2 * h + k, 128, STRIDE), :] = piece[
                    128 * h : 128 * h + 128, 128 * k : 128 * k + 128
                ]
    for g in range(GROUP):
        for y in range(2):
            at = (2 * taken(g) + y) * STRIDE
            out[seat(g), 64 * y : 64 * y + 64, :] = pieces[at : at + 64, :].astype(BF)


def rest_kernel(place, filled, acc, other, label_rows, out, rows, sem):
    half = 3 * ((place[0] >> 1) & 1)
    sub = lax.broadcasted_iota(jnp.int32, (8, 128), 0)
    labels = label_rows[...]
    top = sub < 4
    for i in range(GROUP // 2):
        first, mid, last = (
            [
                acc[6 * (row // 128) + j + half, row % 128 : row % 128 + 8, :]
                + other[3 * (row // 128) + j, row % 128 : row % 128 + 8, :].astype(F32)
                for j in range(3)
            ]
            for row in (24 * i, 24 * i + 8, 24 * i + 16)
        )
        moved = [pltpu.roll(m, 4, 0) for m in mid]
        even = first + [jnp.where(top, mid[0], moved[1]), jnp.where(top, mid[2], labels)]
        odd = last + [jnp.where(top, moved[0], mid[1]), jnp.where(top, moved[2], labels)]
        rows[seat(2 * i)] = jnp.concatenate(even, 0).astype(BF)
        rows[seat(2 * i + 1)] = jnp.concatenate(odd, 0).astype(BF)
    copy = pltpu.make_async_copy(rows, out.at[:, 128:ROWS1], sem)
    copy.start()
    copy.wait()


def place_kernel(got, out, acc):
    lane = lax.broadcasted_iota(jnp.int32, (1, 128), 1)
    cell = lax.broadcasted_iota(jnp.int32, (384, 128), 0)

    def hot(i):
        first = got[2 * i, 160:168, :].astype(F32)
        second = got[2 * i + 1, 160:168, :].astype(F32)
        both = jnp.where(lane < 64, first, second)
        target = both[4:5] * 24.0 + both[5:6] * 4.0 + both[6:7]
        return (cell == target.astype(jnp.int32)).astype(BF)

    for q in range(8):
        eight = slice(8 * q, 8 * q + 8)
        rows = jnp.concatenate([hot(i) for i in range(4 * q, 4 * q + 4)], 1)
        data = jnp.concatenate(
            [got[eight, 0:64, :].reshape(512, 128), got[eight, 64:128, :].reshape(512, 128)], 1
        )
        part = dot10(rows, data)
        acc[...] = part if q == 0 else acc[...] + part
    lanes8 = lax.broadcasted_iota(jnp.int32, (8, 128), 1)
    for half in range(2):
        mine = [g for g in range(GROUP) if (g // 8) % 2 == half]
        total = got[mine[0], 128:168, :].astype(F32)
        for g in mine[1:]:
            total = total + got[g, 128:168, :].astype(F32)
        whole = [total[0:8], total[8:16], total[16:24]]
        part = [total[24:32], pltpu.roll(total[24:32], 4, 0), total[32:40]]
        for z in range(4):
            at = 4 * half + z
            rows = [acc[48 * at : 48 * at + 48, 0:128], acc[48 * at : 48 * at + 48, 128:256]]
            for a, b, c in (whole, part):
                if z == 0:
                    rows.append(a)
                elif z == 1:
                    rows.append(
                        jnp.where(lanes8 < 32, pltpu.roll(a, 32, 1), pltpu.roll(b, 32, 1))
                    )
                elif z == 2:
                    rows.append(
                        jnp.where(lanes8 < 64, pltpu.roll(b, 64, 1), pltpu.roll(c, 64, 1))
                    )
                else:
                    rows.append(pltpu.roll(c, 96, 1))
            out[at] = jnp.concatenate(rows, 0).astype(BF)


def column_kernel(place, got, out):
    total = got[0].astype(F32)
    for z in range(1, 8):
        total = total + got[z].astype(F32)
    sub = lax.broadcasted_iota(jnp.int32, (8, 128), 0)
    lane = lax.broadcasted_iota(jnp.int32, (8, 128), 1)
    tiles = []
    for i in range(6):
        a, b = total[8 * i : 8 * i + 8], total[48 + 8 * i : 56 + 8 * i]
        tiles.append(jnp.where(sub < 4, a, pltpu.roll(b, 4, 0)))
        tiles.append(jnp.where(sub < 4, pltpu.roll(a, 4, 0), b))
    p = place[0] >> 1
    column = 4 * ((6 * p + 8 + (p >> 4)) & 31) + 2 * (place[0] & 1)
    own = 8 * (p & 7) + 2 * (p >> 3)
    whole, part = total[96:104], total[104:112]
    packed = [
        jnp.where(lane < 64, whole, pltpu.roll(part, 64, 1)),
        jnp.where(lane < 64, pltpu.roll(whole, 80, 1), pltpu.roll(part, 16, 1)),
    ]
    for low in range(2):
        for p in range(32):
            b_first, b_last = (24 * p) // 128, (24 * p + 23) // 128
            tile = tiles[6 * low + b_first]
            if b_last != b_first:
                tile = jnp.where(column >= 24 * p - 128 * b_first, tile, tiles[6 * low + b_last])
            out[seat(2 * p + low)] = tile.astype(BF)
    for low in range(2):
        out[own + low] = packed[low].astype(BF)


def final_kernel(place, got, aux_out, virt_out, *, scale):
    p = place[0] >> 1
    for j in range(12):
        q = (6 * p + j // 2) & 31
        odd = q & 1
        holder = 16 * odd + ((11 * (((q - odd) >> 1) + 12)) & 15)
        tile = got[8 * (holder & 7) + 2 * (holder >> 3) + j % 2].astype(F32) * scale
        for y in range(2):
            for o in range(ABPO):
                aux_out[2 * j + y : 2 * j + y + 1, 128 * o : 128 * o + 128] = tile[
                    4 * y + o : 4 * y + o + 1
                ]
    sub = lax.broadcasted_iota(jnp.int32, (8, 128), 0)
    own = 8 * (p & 7) + 2 * (p >> 3)
    first = got[own].astype(F32) * scale
    last = got[own + 1].astype(F32) * scale
    mid = jnp.where(sub < 4, pltpu.roll(first, 64, 1), pltpu.roll(pltpu.roll(last, 64, 1), 4, 0))
    virt_out[0:8, :] = first[:, 0:48]
    virt_out[8:16, :] = mid[:, 0:48]
    virt_out[16:24, :] = last[:, 0:48]


def in_vmem(x):
    return pltpu.with_memory_space_constraint(x, pltpu.VMEM)


def in_hbm(x):
    return pltpu.with_memory_space_constraint(x, pltpu.HBM)


def call(body, ins, outs, scalars=(), scratch=(), held=(), in_place=None):
    smem = pl.BlockSpec(memory_space=pltpu.SMEM)
    vmem = pl.BlockSpec(memory_space=pltpu.VMEM)
    hbm = pl.BlockSpec(memory_space=pltpu.HBM)
    some = pl.BlockSpec(memory_space=pl.ANY)
    lead = [] if in_place is None else [in_place]
    return pl.pallas_call(
        body,
        in_specs=[smem] * len(scalars) + [some] * len(lead) + [hbm] * len(held) + [vmem] * len(ins),
        out_specs=[some if lead else vmem] * len(outs),
        out_shape=outs,
        scratch_shapes=scratch,
        input_output_aliases={len(scalars): 0} if lead else {},
        compiler_params=VMEM,
    )(*scalars, *lead, *map(in_hbm, held), *map(in_vmem, ins))


def on_device(integrals, amplitudes, pno_density, pno_coef, pao_blocks, aux_slice, aux_offset):
    pair = 8 * lax.axis_index("y") + lax.axis_index("x")
    place = [(2 * pair + lax.axis_index("low")).reshape(1)]
    scale = 1.0 / math.sqrt(PAIRS * 32)
    sds = jax.ShapeDtypeStruct
    names = pltpu.SMEM((2, PAIRS), jnp.int32)
    acc, other, coef, ints, amps, labels = call(
        virtual_kernel,
        [],
        [
            sds((36, 128, 128), F32),
            sds((18, 128, 128), BF),
            sds((PAIRS, 64, 256), BF),
            sds((PAIRS, 64, 256), BF),
            sds((PAIRS, 64, 64), BF),
            sds((8, 128), F32),
        ],
        place,
        [
            pltpu.VMEM((PAIRS, 64, 64), BF),
            pltpu.VMEM((PAIRS, 64, 256), BF),
            names,
            names,
            names,
            pltpu.SemaphoreType.DMA((7,)),
        ],
        held=[
            pno_density,
            jnp.swapaxes(pno_coef, 1, 2),
            pao_blocks.T,
            aux_slice.T,
            aux_offset.T,
            jnp.swapaxes(integrals, 1, 2),
            amplitudes,
        ],
    )
    other = lax.ppermute(other, ("y", "x"), [(i, i ^ 1) for i in range(32)])
    (filled,) = call(
        piece_kernel,
        [ints, amps, coef],
        [sds((GROUP, ROWS1, 128), BF)],
        scratch=[pltpu.VMEM((128 * STRIDE, 128), F32), pltpu.VMEM((PAIRS, 64, 256), BF)],
    )
    (sent,) = call(
        rest_kernel,
        [acc, other, labels],
        [sds((GROUP, ROWS1, 128), BF)],
        place,
        scratch=[pltpu.VMEM((GROUP, ROWS1 - 128, 128), BF), pltpu.SemaphoreType.DMA(())],
        in_place=filled,
    )
    got = lax.all_to_all(sent, ("x", "y", "low"), split_axis=0, concat_axis=0, tiled=True)
    (sent,) = call(
        place_kernel,
        [got],
        [sds((8, ROWS2, 128), BF)],
        [],
        scratch=[pltpu.VMEM((384, 256), F32)],
    )
    got = lax.all_to_all(sent, "high", split_axis=0, concat_axis=0, tiled=True)
    (sent,) = call(
        column_kernel,
        [got],
        [sds((GROUP, 8, 128), BF)],
        place,
    )
    got = lax.all_to_all(sent, ("x", "y", "low"), split_axis=0, concat_axis=0, tiled=True)
    aux, virt = call(
        lambda *refs: final_kernel(*refs, scale=scale),
        [got],
        [sds((24, 512), F32), sds((24, 48), F32)],
        place,
    )
    return aux.T, virt.T


def solution(mesh):
    every = ("y", "x", "high", "low")
    split = Mesh(mesh.devices.reshape(4, 8, 8, 2), every)
    in_specs = (P(every, None, None),) * 4 + (P(every, None),) * 3
    out_specs = (P(("high", "low"), ("y", "x")),) * 2
    return jax.shard_map(
        on_device, mesh=split, in_specs=in_specs, out_specs=out_specs, check_vma=False
    )
```
